32 devices in a mesh: tm: 4 (over y, x), seq: 8 (over z, core).
Axes of the slice: x: 2, y: 2, z: 4, core: 2. Of those that a mesh axis runs over, the one named last changes fastest.
Arguments:
- queries: bfloat16 [4, 1024, 1024], P('tm', 'seq'), may hold values from -5 to 5
- keys: bfloat16 [4, 1024, 1024], P('tm', 'seq'), may hold values from -5 to 5
- values: bfloat16 [4, 1024, 1024], P('tm', 'seq'), may hold values from -6 to 6
- grad_out: bfloat16 [4, 1024, 1024], P('tm', 'seq'), may hold values from -6 to 6
- block_mask: int32 [4, 8, 6], P('tm', 'seq'), may hold values from 0 to 1, as said below
- valid_len: int32 [4], replicated, may hold values from 512 to 1024, as said below
Outputs:
- grad_query: bfloat16 [4, 1024, 1024], P('tm', 'seq')
- grad_key: bfloat16 [4, 1024, 1024], P('tm', 'seq')
- grad_value: bfloat16 [4, 1024, 1024], P('tm', 'seq')
The draws below stay inside these ranges and needn't reach their ends.
Inputs may be any that keep to these rules, and one draw needn't show every extreme that they name: `block_mask`: entry 1 (a query block's own block) is always 1. `valid_len`: some frame is complete.
All inputs are finite; a program needn't handle non-finite values.
Results may differ from the reference program's by a relative error of at most 0.022.
Values may be sent and summed in bfloat16 or wider, within the bound.
A program may use at most 64 MiB of HBM per device.

```python
import jax
import jax.numpy as jnp
from jax import lax

HEADS = 8
HD = 128
BLK = 128
FRAMES = 4
NBLK = 8
FRAME_TOK = 1024
FEAT = 1024


def draw_queries(key, part):
    array_dims = (FRAMES, NBLK, BLK, HEADS * HD)
    sample = jnp.clip(jax.random.normal(jax.random.fold_in(key, 1), array_dims, jnp.float32), -4.5, 4.5)
    return sample.reshape(FRAMES, FRAME_TOK, HEADS * HD).astype(jnp.bfloat16)


def draw_keys(key, part):
    array_dims = (FRAMES, NBLK, BLK, HEADS * HD)
    sample = jnp.clip(jax.random.normal(jax.random.fold_in(key, 2), array_dims, jnp.float32), -4.5, 4.5)
    return sample.reshape(FRAMES, FRAME_TOK, HEADS * HD).astype(jnp.bfloat16)


def draw_block_mask(key, part):
    coin_flips = jax.random.randint(jax.random.fold_in(key, 5), (FRAMES, NBLK, 6), 0, 2)
    own_entry = (jnp.arange(6) == 1)[None, None, :]
    return jnp.where(own_entry, 1, coin_flips).astype(jnp.int32)


def draw_valid_len(key, part):
    counts = jax.random.randint(jax.random.fold_in(key, 3), (FRAMES,), FRAME_TOK // 2, FRAME_TOK + 1)
    complete = jax.random.randint(jax.random.fold_in(key, 4), (), 0, FRAMES)
    return jnp.where(jnp.arange(FRAMES) == complete, FRAME_TOK, counts).astype(jnp.int32)


def block_levels(own_key, extent, shards, smallest, largest):
    gain = 1.0
    for position, parts in shards:
        draws = jax.random.uniform(jax.random.fold_in(jax.random.fold_in(own_key, 6), position), (parts,), jnp.float32, smallest / len(shards), largest / len(shards))
        gain = gain * jnp.repeat(jnp.exp(draws), extent[position] // parts).reshape((-1,) + (1,) * (len(extent) - 1 - position))
    return gain


def gaussian(key, dims, deviation, bound, shards=(), kind=jnp.bfloat16):
    values = jax.random.normal(key, dims, jnp.float32) * deviation
    if len(shards) > 0:
        values = block_levels(key, dims, shards, -0.22, 0.18) * values
    return jnp.clip(values, min=-bound, max=bound).astype(kind)


def setup_inputs(seed: int = 0) -> dict:
    key_list = jax.random.split(jax.random.key(seed), 7)
    queries = draw_queries(jax.random.fold_in(key_list[6], 71), 0)
    keys = draw_keys(jax.random.fold_in(key_list[6], 71), 0)
    values = gaussian(key_list[2], (FRAMES, FRAME_TOK, FEAT), 1.0, 6.0, ((0, 4), (1, 8)))
    grad_out = gaussian(key_list[3], (FRAMES, FRAME_TOK, FEAT), 1.0, 6.0, ((0, 4), (1, 8)))
    block_mask = draw_block_mask(jax.random.fold_in(key_list[6], 71), 0)
    valid_len = draw_valid_len(jax.random.fold_in(key_list[6], 71), 0)
    return dict(queries=queries, keys=keys, values=values, grad_out=grad_out, block_mask=block_mask, valid_len=valid_len)


def attend_block(query_blk, key_ext, value_ext, grad_blk, allowed, query_ok):
    feat_dim = query_blk.shape[-1]
    head_dim = feat_dim // HEADS
    scaling = head_dim ** -0.5
    query_heads = query_blk.astype(jnp.float32).reshape(BLK, HEADS, head_dim)
    key_heads = key_ext.astype(jnp.float32).reshape(6 * BLK, HEADS, head_dim)
    value_heads = value_ext.astype(jnp.float32).reshape(6 * BLK, HEADS, head_dim)
    scores = scaling * jnp.einsum('ihd,jhd->hij', query_heads, key_heads)
    masked = jnp.where(allowed[None, None, :], scores, -1e30)
    row_max = jnp.max(masked, axis=-1, keepdims=True)
    log_total = row_max + jnp.log(jnp.sum(jnp.exp(masked - row_max), axis=-1, keepdims=True))
    prob_f32 = jnp.exp(masked - log_total)
    prob_bf = lax.optimization_barrier(prob_f32.astype(jnp.bfloat16)).astype(jnp.float32)
    attended = jnp.einsum('hij,jhd->ihd', prob_bf, value_heads)
    okay = query_ok.astype(jnp.float32)[:, None, None]
    attended_bf = lax.optimization_barrier((attended * okay).astype(jnp.bfloat16)).astype(jnp.float32)
    grad_in = grad_blk.astype(jnp.float32).reshape(BLK, HEADS, head_dim) * okay
    row_dot = jnp.sum(grad_in * attended_bf, axis=-1)
    dprob = jnp.einsum('ihd,jhd->hij', grad_in, value_heads)
    dscore = prob_f32 * (dprob - jnp.transpose(row_dot)[:, :, None])
    dscore = lax.optimization_barrier(dscore.astype(jnp.bfloat16)).astype(jnp.float32)
    grad_query = (scaling * jnp.einsum('hij,jhd->ihd', dscore, key_heads)).astype(jnp.bfloat16)
    grad_key = scaling * jnp.einsum('hij,ihd->jhd', dscore, query_heads)
    grad_value = jnp.einsum('hij,ihd->jhd', prob_bf, grad_in)
    return (grad_query.reshape(BLK, feat_dim), grad_key.reshape(6 * BLK, feat_dim),
            grad_value.reshape(6 * BLK, feat_dim))


def reference(queries, keys, values, grad_out, block_mask, valid_len):
    frames = queries.shape[0]
    feat_dim = queries.shape[2]
    blocks_all = queries.shape[1] // BLK

    def split(array):
        return array.reshape(frames, blocks_all, BLK, feat_dim)

    key_pad = jnp.pad(split(keys), ((1, 0), (1, 1), (0, 0), (0, 0)))
    value_pad = jnp.pad(split(values), ((1, 0), (1, 1), (0, 0), (0, 0)))
    query_blocks = split(queries)
    grad_blocks = split(grad_out)
    candidate = jnp.arange(6, dtype=jnp.int32)
    inside = jnp.arange(BLK, dtype=jnp.int32)
    zero = jnp.zeros((), jnp.int32)

    def add_at(accum, piece, frame_pos, block_pos):
        start = (frame_pos, block_pos, zero, zero)
        current = lax.dynamic_slice(accum, start, (1, 3, BLK, feat_dim))
        return lax.dynamic_update_slice(accum, current + piece[None], start)

    def neighbours(padded, frame_idx, block_idx):
        own_part = lax.dynamic_slice(padded, (frame_idx + 1, block_idx, zero, zero), (1, 3, BLK, feat_dim))[0]
        prev_part = lax.dynamic_slice(padded, (frame_idx, block_idx, zero, zero), (1, 3, BLK, feat_dim))[0]
        return jnp.concatenate((own_part, prev_part), axis=0).reshape(6 * BLK, feat_dim)

    def step(carry, step_index):
        key_acc, value_acc = carry
        frame_idx = step_index // blocks_all
        block_idx = step_index % blocks_all
        query_blk = query_blocks[frame_idx, block_idx]
        grad_blk = grad_blocks[frame_idx, block_idx]
        key_ext = neighbours(key_pad, frame_idx, block_idx)
        value_ext = neighbours(value_pad, frame_idx, block_idx)
        near_block = block_idx + candidate % 3 - 1
        src_frame = frame_idx - candidate // 3
        src_valid = valid_len[jnp.clip(src_frame, 0, frames - 1)]
        positions = near_block[:, None] * BLK + inside[None, :]
        block_ok = (block_mask[frame_idx, block_idx] == 1) & (near_block >= 0) & (near_block < blocks_all) & (src_frame >= 0)
        allowed = (block_ok[:, None] & (positions < src_valid[:, None])).reshape(6 * BLK)
        query_ok = block_idx * BLK + inside < valid_len[frame_idx]
        grad_query, grad_key, grad_value = attend_block(query_blk, key_ext, value_ext, grad_blk, allowed, query_ok)
        grad_key = grad_key.reshape(2, 3, BLK, feat_dim)
        grad_value = grad_value.reshape(2, 3, BLK, feat_dim)
        key_acc = add_at(add_at(key_acc, grad_key[0], frame_idx + 1, block_idx), grad_key[1], frame_idx, block_idx)
        value_acc = add_at(add_at(value_acc, grad_value[0], frame_idx + 1, block_idx), grad_value[1], frame_idx, block_idx)
        return (key_acc, value_acc), grad_query

    start_acc = jnp.zeros(key_pad.shape, jnp.float32)
    (key_acc, value_acc), query_parts = lax.scan(step, (start_acc, start_acc), jnp.arange(frames * blocks_all, dtype=jnp.int32))
    grad_query = query_parts.reshape(frames, blocks_all * BLK, feat_dim)
    grad_key = key_acc[1:, 1:-1].reshape(frames, blocks_all * BLK, feat_dim).astype(jnp.bfloat16)
    grad_value = value_acc[1:, 1:-1].reshape(frames, blocks_all * BLK, feat_dim).astype(jnp.bfloat16)
    return (grad_query, grad_key, grad_value)
```

```python
import functools
import math

import jax
import jax.numpy as jnp
from jax import lax
from jax.experimental import pallas as pl
from jax.experimental.pallas import tpu as pltpu
from jax.sharding import PartitionSpec as P

HEADS = 8
RING = 3
LAG_GRADS = 2
LAG_SUMS = 4
BIG = 1e30
MESH = pl.DeviceIdType.MESH
NT = (((1,), (1,)), ((), ()))
TN = (((0,), (0,)), ((), ()))
NN = (((1,), (0,)), ((), ()))


def dot(a, b, dims):
    return lax.dot_general(a, b, dims, preferred_element_type=jnp.float32)


def kernel(
    frames, blocks, block_len, head_dim,
    k_in, v_in, q_in, g_in, mask_ref, valid_ref,
    dq_ref, dk_ref, dv_ref,
    kv, qg, bias, gate, e_ring, d_ring, stat, stat_far, dq_home, dk_home, dv_home,
    dq_out, dq_far, dkv_out, dkv_far,
    own_sem, kv_send, kv_recv, qg_send, qg_recv, gate_sem, stat_send, stat_recv, dq_send, dq_recv, dkv_send, dkv_recv,
):
    n = block_len
    t = lax.axis_index("tm")
    s = lax.axis_index("seq")
    scale = head_dim ** (-0.5)
    scale2 = scale * math.log2(math.e)
    left, right = s > 0, s < blocks - 1
    earlier, later = t > 0, t < frames - 1
    sides = ((left, -1), (right, 1))

    def cols(h):
        return pl.ds(pl.multiple_of(h * head_dim, head_dim), head_dim)

    def remote(src, dst, send, recv, dt, ds):
        return pltpu.make_async_remote_copy(
            src_ref=src, dst_ref=dst, send_sem=send, recv_sem=recv,
            device_id=(t + dt, s + ds), device_id_type=MESH,
        )

    def kv_copy(h, side):
        slot = 2 - 2 * side
        return remote(
            kv.at[:, n:2 * n, cols(h)], kv.at[:, slot * n:(slot + 1) * n, cols(h)],
            kv_send.at[side, h], kv_recv.at[side, h], 0, (-1, 1)[side],
        )

    def qg_copy(h):
        return remote(qg.at[:, :n, cols(h)], qg.at[:, n:, cols(h)], qg_send.at[h], qg_recv.at[h], -1, 0)

    def gate_copy():
        return remote(gate.at[0], gate.at[1], gate_sem.at[0], gate_sem.at[1], -1, 0)

    def stat_copy(h, up):
        src, dst = ((slice(0, n), slice(n, 2 * n)), (slice(n, 2 * n), slice(0, n)))[up]
        return remote(
            stat.at[h, :, src], stat_far.at[h, :, dst], stat_send.at[up, h], stat_recv.at[up, h], (-1, 1)[up], 0
        )

    def dq_copy(h):
        return remote(dq_out.at[h], dq_far.at[h], dq_send.at[h], dq_recv.at[h], 1, 0)

    def dkv_copy(h, side):
        return remote(
            dkv_out.at[side, h], dkv_far.at[side, h], dkv_send.at[side, h], dkv_recv.at[side, h], 0, (-1, 1)[side]
        )

    barrier = pltpu.get_barrier_semaphore()
    expected = jnp.int32(0)
    for there, dt, ds in ((left, 0, -1), (right, 0, 1), (earlier, -1, 0), (later, 1, 0)):
        expected = expected + there.astype(jnp.int32)

        @pl.when(there)
        def _(dt=dt, ds=ds):
            pl.semaphore_signal(barrier, inc=1, device_id=(t + dt, s + ds), device_id_type=MESH)

    own = [
        pltpu.make_async_copy(k_in.at[0], kv.at[0, n:2 * n], own_sem.at[0]),
        pltpu.make_async_copy(v_in.at[0], kv.at[1, n:2 * n], own_sem.at[1]),
        pltpu.make_async_copy(q_in.at[0], qg.at[0, :n], own_sem.at[2]),
        pltpu.make_async_copy(g_in.at[0], qg.at[1, :n], own_sem.at[3]),
    ]
    for c in own:
        c.start()

    for c in range(3):
        gate[0, c:c + 1, :] = jnp.full((1, n), jnp.where(mask_ref[0, 0, 3 + c] == 1, 1.0, 0.0), jnp.float32)

    row = lax.broadcasted_iota(jnp.int32, (n, n), 0)
    frame_valid = valid_ref[t]

    def key_limit(c):
        near = s + c - 1
        inside = jnp.logical_and(near >= 0, near < blocks).astype(jnp.int32)
        return jnp.maximum(frame_valid - near * n, 0) * inside

    for c in range(3):
        limit = key_limit(c) * jnp.where(mask_ref[0, 0, c] == 1, 1, 0)
        bias[c * n:(c + 1) * n, :n] = jnp.where(row < limit, 0.0, -BIG)

    lane = lax.broadcasted_iota(jnp.int32, (1, 2 * n), 1)
    next_valid = valid_ref[jnp.minimum(t + 1, frames - 1)] * later.astype(jnp.int32)
    okay = jnp.where(lane < jnp.where(lane < n, jnp.minimum(frame_valid - s * n, n), next_valid - s * n + n), 1.0, 0.0)

    zeros = jnp.zeros((n, kv.shape[2]), kv.dtype)
    none = jnp.where(lax.broadcasted_iota(jnp.int32, (8, n), 0) == 0, -BIG, 0.0)
    for slot, there in ((0, left), (2, right)):
        @pl.when(jnp.logical_not(there))
        def _(slot=slot):
            for k in range(2):
                kv[k, slot * n:(slot + 1) * n, :] = zeros
            dkv_far[1 - slot // 2] = jnp.zeros(dkv_far.shape[1:], dkv_far.dtype)

    @pl.when(jnp.logical_not(later))
    def _():
        for k in range(2):
            qg[k, n:, :] = zeros
        gate[1] = jnp.zeros((8, n), jnp.float32)
        for h in range(HEADS):
            stat_far[h, :, n:] = none

    @pl.when(jnp.logical_not(earlier))
    def _():
        dq_far[...] = jnp.zeros(dq_far.shape, dq_far.dtype)
        for h in range(HEADS):
            stat_far[h, :, :n] = none

    for c in own:
        c.wait()
    pl.semaphore_wait(barrier, expected)

    @pl.when(earlier)
    def _():
        gate_copy().start()

    @pl.loop(0, HEADS)
    def _(h):
        @pl.when(earlier)
        def _():
            qg_copy(h).start()

        for side, (there, _) in enumerate(sides):
            @pl.when(there)
            def _(side=side):
                kv_copy(h, side).start()

    @pl.when(later)
    def _():
        gate_copy().wait_recv()

    for c in range(3):
        open_here = jnp.logical_and(row < key_limit(c), gate[1, c:c + 1, :] > 0.5)
        bias[c * n:(c + 1) * n, n:] = jnp.where(open_here, 0.0, -BIG)

    def scores(h):
        for side, (there, _) in enumerate(sides):
            @pl.when(there)
            def _(side=side):
                kv_copy(h, 1 - side).wait_recv()

        @pl.when(later)
        def _():
            qg_copy(h).wait_recv()

        hc = cols(h)
        slot = lax.rem(h, RING)
        score = dot(kv[0, :, hc], qg[0, :, hc], NT) * scale2 + bias[...]
        peak = jnp.max(score, axis=0, keepdims=True)
        e = jnp.exp2(score - peak)
        dprob = dot(kv[1, :, hc], qg[1, :, hc], NT)
        e_ring[slot] = e
        d_ring[slot] = dprob
        stat[h, 0:1, :] = peak
        stat[h, 1:2, :] = jnp.sum(e, axis=0, keepdims=True)
        stat[h, 2:3, :] = jnp.sum(e * dprob, axis=0, keepdims=True)

        @pl.when(later)
        def _():
            stat_copy(h, 1).start()

        @pl.when(earlier)
        def _():
            stat_copy(h, 0).start()

    def grads(h):
        @pl.when(earlier)
        def _():
            stat_copy(h, 1).wait_recv()

        @pl.when(later)
        def _():
            stat_copy(h, 0).wait_recv()

        hc = cols(h)
        slot = lax.rem(h, RING)
        near, far = stat[h], stat_far[h]
        peak = jnp.maximum(near[0:1], far[0:1])
        a, b = jnp.exp2(near[0:1] - peak), jnp.exp2(far[0:1] - peak)
        norm = 1.0 / (near[1:2] * a + far[1:2] * b)
        row_dot = (near[2:3] * a + far[2:3] * b) * norm
        prob = e_ring[slot] * (okay * a * norm)
        dscore = (prob * (d_ring[slot] - row_dot)).astype(jnp.bfloat16)
        query, grad, key = qg[0, :, hc], qg[1, :, hc], kv[0, :, hc]
        dq = dot(dscore, key, TN) * scale
        dq_home[:, hc] = dq[:n]
        dq_out[h] = dq[n:].astype(dq_out.dtype)

        @pl.when(later)
        def _():
            dq_copy(h).start()

        dk = dot(dscore, query, NN) * scale
        dv = dot(prob.astype(jnp.bfloat16), grad, NN)
        dk_home[:, hc] = dk[n:2 * n]
        dv_home[:, hc] = dv[n:2 * n]
        for side, (there, _) in enumerate(sides):
            part = slice(2 * side * n, (2 * side + 1) * n)
            dkv_out[side, h, :n] = dk[part].astype(dkv_out.dtype)
            dkv_out[side, h, n:] = dv[part].astype(dkv_out.dtype)

            @pl.when(there)
            def _(side=side):
                dkv_copy(h, side).start()

    def sums(h):
        hc = cols(h)

        @pl.when(earlier)
        def _():
            dq_copy(h).wait_recv()

        dq_ref[0, :, hc] = (dq_home[:, hc] + dq_far[h].astype(jnp.float32)).astype(dq_ref.dtype)
        for side, (there, _) in enumerate(sides):
            @pl.when(there)
            def _(side=side):
                dkv_copy(h, 1 - side).wait_recv()
        from_right, from_left = dkv_far[0, h].astype(jnp.float32), dkv_far[1, h].astype(jnp.float32)
        both = from_right + from_left
        dk_ref[0, :, hc] = (dk_home[:, hc] + both[:n]).astype(dk_ref.dtype)
        dv_ref[0, :, hc] = (dv_home[:, hc] + both[n:]).astype(dv_ref.dtype)

    @pl.loop(0, HEADS + LAG_SUMS)
    def _(i):
        @pl.when(i < HEADS)
        def _():
            scores(i)

        @pl.when(jnp.logical_and(i >= LAG_GRADS, i < HEADS + LAG_GRADS))
        def _():
            grads(i - LAG_GRADS)

        @pl.when(i >= LAG_SUMS)
        def _():
            sums(i - LAG_SUMS)

    @pl.when(earlier)
    def _():
        gate_copy().wait_send()

    @pl.loop(0, HEADS)
    def _(h):
        @pl.when(earlier)
        def _():
            qg_copy(h).wait_send()
            stat_copy(h, 0).wait_send()

        @pl.when(later)
        def _():
            stat_copy(h, 1).wait_send()
            dq_copy(h).wait_send()

        for side, (there, _) in enumerate(sides):
            @pl.when(there)
            def _(side=side):
                kv_copy(h, side).wait_send()
                dkv_copy(h, side).wait_send()


def solution(mesh):
    frames, blocks = mesh.shape["tm"], mesh.shape["seq"]

    def body(queries, keys, values, grad_out, block_mask, valid_len):
        _, n, feat = queries.shape
        hd = feat // HEADS
        out = jax.ShapeDtypeStruct(queries.shape, queries.dtype)
        vmem = pl.BlockSpec(memory_space=pltpu.VMEM)
        smem = pl.BlockSpec(memory_space=pltpu.SMEM)
        hbm = pl.BlockSpec(memory_space=pl.ANY)
        dma = pltpu.SemaphoreType.DMA
        return pl.pallas_call(
            functools.partial(kernel, frames, blocks, n, hd),
            out_shape=(out, out, out),
            in_specs=[hbm] * 4 + [smem] * 2,
            out_specs=(vmem,) * 3,
            scratch_shapes=[
                pltpu.VMEM((2, 3 * n, feat), jnp.bfloat16),
                pltpu.VMEM((2, 2 * n, feat), jnp.bfloat16),
                pltpu.VMEM((3 * n, 2 * n), jnp.float32),
                pltpu.VMEM((2, 8, n), jnp.float32),
                pltpu.VMEM((RING, 3 * n, 2 * n), jnp.float32),
                pltpu.VMEM((RING, 3 * n, 2 * n), jnp.float32),
                pltpu.VMEM((HEADS, 8, 2 * n), jnp.float32),
                pltpu.VMEM((HEADS, 8, 2 * n), jnp.float32),
                pltpu.VMEM((n, feat), jnp.float32),
                pltpu.VMEM((n, feat), jnp.float32),
                pltpu.VMEM((n, feat), jnp.float32),
                pltpu.VMEM((HEADS, n, hd), jnp.bfloat16),
                pltpu.VMEM((HEADS, n, hd), jnp.bfloat16),
                pltpu.VMEM((2, HEADS, 2 * n, hd), jnp.bfloat16),
                pltpu.VMEM((2, HEADS, 2 * n, hd), jnp.bfloat16),
                dma((4,)),
                dma((2, HEADS)),
                dma((2, HEADS)),
                dma((HEADS,)),
                dma((HEADS,)),
                dma((2,)),
                dma((2, HEADS)),
                dma((2, HEADS)),
                dma((HEADS,)),
                dma((HEADS,)),
                dma((2, HEADS)),
                dma((2, HEADS)),
            ],
            compiler_params=pltpu.CompilerParams(collective_id=0, has_side_effects=True),
        )(keys, values, queries, grad_out, block_mask, valid_len)

    spec = P("tm", "seq", None)
    return jax.shard_map(
        body, mesh=mesh, in_specs=(spec,) * 5 + (P(),), out_specs=(spec,) * 3, check_vma=False
    )
```

```python
import functools
import math

import jax
import jax.numpy as jnp
from jax import lax
from jax.experimental import pallas as pl
from jax.experimental.pallas import tpu as pltpu
from jax.sharding import PartitionSpec as P

HEADS = 8
AHEAD = 4
LAG_GRADS = 4
LAG_SUMS = 7
RING = LAG_GRADS + 1
BIG = 1e30
MESH = pl.DeviceIdType.MESH
NT = (((1,), (1,)), ((), ()))
TN = (((0,), (0,)), ((), ()))
NN = (((1,), (0,)), ((), ()))


def dot(a, b, dims):
    return lax.dot_general(a, b, dims, preferred_element_type=jnp.float32)


def kernel(
    frames, blocks, block_len, head_dim,
    k_in, v_in, q_in, g_in, mask_ref, valid_ref,
    dq_ref, dk_ref, dv_ref,
    kv, qg, bias, gate, e_ring, d_ring, stat, stat_far, dq_home, dk_home, dv_home,
    dq_out, dq_far, dkv_out, dkv_far,
    own_sem, kv_send, kv_recv, qg_send, qg_recv, gate_sem, stat_send, stat_recv, dq_send, dq_recv, dkv_send, dkv_recv,
):
    n = block_len
    t = lax.axis_index("tm")
    s = lax.axis_index("seq")
    scale = head_dim ** (-0.5)
    scale2 = scale * math.log2(math.e)
    left, right = s > 0, s < blocks - 1
    earlier, later = t > 0, t < frames - 1
    sides = ((left, -1), (right, 1))

    def cols(h):
        return pl.ds(pl.multiple_of(h * head_dim, head_dim), head_dim)

    def remote(src, dst, send, recv, dt, ds):
        return pltpu.make_async_remote_copy(
            src_ref=src, dst_ref=dst, send_sem=send, recv_sem=recv,
            device_id=(t + dt, s + ds), device_id_type=MESH,
        )

    def kv_copy(h, side):
        slot = 2 - 2 * side
        return remote(
            kv.at[:, n:2 * n, cols(h)], kv.at[:, slot * n:(slot + 1) * n, cols(h)],
            kv_send.at[side, h], kv_recv.at[side, h], 0, (-1, 1)[side],
        )

    def qg_copy(h):
        return remote(qg.at[:, :n, cols(h)], qg.at[:, n:, cols(h)], qg_send.at[h], qg_recv.at[h], -1, 0)

    def gate_copy():
        return remote(gate.at[0], gate.at[1], gate_sem.at[0], gate_sem.at[1], -1, 0)

    def stat_copy(h, up):
        src, dst = ((slice(0, n), slice(n, 2 * n)), (slice(n, 2 * n), slice(0, n)))[up]
        return remote(
            stat.at[h, :, src], stat_far.at[h, :, dst], stat_send.at[up, h], stat_recv.at[up, h], (-1, 1)[up], 0
        )

    def dq_copy(h):
        return remote(dq_out.at[h], dq_far.at[h], dq_send.at[h], dq_recv.at[h], 1, 0)

    def dkv_copy(h, side):
        return remote(
            dkv_out.at[side, h], dkv_far.at[side, h], dkv_send.at[side, h], dkv_recv.at[side, h], 0, (-1, 1)[side]
        )

    barrier = pltpu.get_barrier_semaphore()
    expected = jnp.int32(0)
    for there, dt, ds in ((left, 0, -1), (right, 0, 1), (earlier, -1, 0), (later, 1, 0)):
        expected = expected + there.astype(jnp.int32)

        @pl.when(there)
        def _(dt=dt, ds=ds):
            pl.semaphore_signal(barrier, inc=1, device_id=(t + dt, s + ds), device_id_type=MESH)

    own = [
        pltpu.make_async_copy(k_in.at[0], kv.at[0, n:2 * n], own_sem.at[0]),
        pltpu.make_async_copy(v_in.at[0], kv.at[1, n:2 * n], own_sem.at[1]),
        pltpu.make_async_copy(q_in.at[0], qg.at[0, :n], own_sem.at[2]),
        pltpu.make_async_copy(g_in.at[0], qg.at[1, :n], own_sem.at[3]),
    ]
    for c in own:
        c.start()

    for c in range(3):
        gate[0, c:c + 1, :] = jnp.full((1, n), jnp.where(mask_ref[0, 0, 3 + c] == 1, 1.0, 0.0), jnp.float32)

    row = lax.broadcasted_iota(jnp.int32, (n, n), 0)
    frame_valid = valid_ref[t]

    def key_limit(c):
        near = s + c - 1
        inside = jnp.logical_and(near >= 0, near < blocks).astype(jnp.int32)
        return jnp.maximum(frame_valid - near * n, 0) * inside

    for c in range(3):
        limit = key_limit(c) * jnp.where(mask_ref[0, 0, c] == 1, 1, 0)
        bias[c * n:(c + 1) * n, :n] = jnp.where(row < limit, 0.0, -BIG)

    lane = lax.broadcasted_iota(jnp.int32, (1, 2 * n), 1)
    next_valid = valid_ref[jnp.minimum(t + 1, frames - 1)] * later.astype(jnp.int32)
    okay = jnp.where(lane < jnp.where(lane < n, jnp.minimum(frame_valid - s * n, n), next_valid - s * n + n), 1.0, 0.0)

    zeros = jnp.zeros((n, kv.shape[2]), kv.dtype)
    none = jnp.where(lax.broadcasted_iota(jnp.int32, (8, n), 0) == 0, -BIG, 0.0)
    for slot, there in ((0, left), (2, right)):
        @pl.when(jnp.logical_not(there))
        def _(slot=slot):
            for k in range(2):
                kv[k, slot * n:(slot + 1) * n, :] = zeros
            dkv_far[1 - slot // 2] = jnp.zeros(dkv_far.shape[1:], dkv_far.dtype)

    @pl.when(jnp.logical_not(later))
    def _():
        for k in range(2):
            qg[k, n:, :] = zeros
        gate[1] = jnp.zeros((8, n), jnp.float32)
        for h in range(HEADS):
            stat_far[h, :, n:] = none

    @pl.when(jnp.logical_not(earlier))
    def _():
        dq_far[...] = jnp.zeros(dq_far.shape, dq_far.dtype)
        for h in range(HEADS):
            stat_far[h, :, :n] = none

    for c in own:
        c.wait()
    pl.semaphore_wait(barrier, expected)

    @pl.when(earlier)
    def _():
        gate_copy().start()

    @pl.loop(0, HEADS)
    def _(h):
        @pl.when(jnp.logical_and(earlier, h < AHEAD))
        def _():
            qg_copy(h).start()

        for side, (there, _) in enumerate(sides):
            @pl.when(there)
            def _(side=side):
                kv_copy(h, side).start()

    @pl.when(later)
    def _():
        gate_copy().wait_recv()

    for c in range(3):
        open_here = jnp.logical_and(row < key_limit(c), gate[1, c:c + 1, :] > 0.5)
        bias[c * n:(c + 1) * n, n:] = jnp.where(open_here, 0.0, -BIG)

    def scores(h):
        for side, (there, _) in enumerate(sides):
            @pl.when(there)
            def _(side=side):
                kv_copy(h, 1 - side).wait_recv()

        @pl.when(later)
        def _():
            qg_copy(h).wait_recv()

        hc = cols(h)
        slot = lax.rem(h, RING)
        score = dot(kv[0, :, hc], qg[0, :, hc], NT) * scale2 + bias[...]
        peak = jnp.max(score, axis=0, keepdims=True)
        e = jnp.exp2(score - peak)
        dprob = dot(kv[1, :, hc], qg[1, :, hc], NT)
        e_ring[slot] = e
        d_ring[slot] = dprob
        stat[h, 0:1, :] = peak
        stat[h, 1:2, :] = jnp.sum(e, axis=0, keepdims=True)
        stat[h, 2:3, :] = jnp.sum(e * dprob, axis=0, keepdims=True)

        @pl.when(later)
        def _():
            stat_copy(h, 1).start()

        @pl.when(earlier)
        def _():
            stat_copy(h, 0).start()

    def grads(h):
        @pl.when(earlier)
        def _():
            stat_copy(h, 1).wait_recv()

        @pl.when(later)
        def _():
            stat_copy(h, 0).wait_recv()

        hc = cols(h)
        slot = lax.rem(h, RING)
        near, far = stat[h], stat_far[h]
        peak = jnp.maximum(near[0:1], far[0:1])
        a, b = jnp.exp2(near[0:1] - peak), jnp.exp2(far[0:1] - peak)
        norm = 1.0 / (near[1:2] * a + far[1:2] * b)
        row_dot = (near[2:3] * a + far[2:3] * b) * norm
        prob = e_ring[slot] * (okay * a * norm)
        dscore = (prob * (d_ring[slot] - row_dot)).astype(jnp.bfloat16)
        query, grad, key = qg[0, :, hc], qg[1, :, hc], kv[0, :, hc]
        dq = dot(dscore, key, TN) * scale
        dq_home[:, hc] = dq[:n]
        dq_out[h] = dq[n:].astype(dq_out.dtype)

        @pl.when(later)
        def _():
            dq_copy(h).start()

        dk = dot(dscore, query, NN) * scale
        dv = dot(prob.astype(jnp.bfloat16), grad, NN)
        dk_home[:, hc] = dk[n:2 * n]
        dv_home[:, hc] = dv[n:2 * n]
        for side, (there, _) in enumerate(sides):
            part = slice(2 * side * n, (2 * side + 1) * n)
            dkv_out[side, h, :n] = dk[part].astype(dkv_out.dtype)
            dkv_out[side, h, n:] = dv[part].astype(dkv_out.dtype)

            @pl.when(there)
            def _(side=side):
                dkv_copy(h, side).start()

    def sums(h):
        hc = cols(h)

        @pl.when(earlier)
        def _():
            dq_copy(h).wait_recv()

        dq_ref[0, :, hc] = (dq_home[:, hc] + dq_far[h].astype(jnp.float32)).astype(dq_ref.dtype)
        for side, (there, _) in enumerate(sides):
            @pl.when(there)
            def _(side=side):
                dkv_copy(h, 1 - side).wait_recv()
        from_right, from_left = dkv_far[0, h].astype(jnp.float32), dkv_far[1, h].astype(jnp.float32)
        both = from_right + from_left
        dk_ref[0, :, hc] = (dk_home[:, hc] + both[:n]).astype(dk_ref.dtype)
        dv_ref[0, :, hc] = (dv_home[:, hc] + both[n:]).astype(dv_ref.dtype)

    @pl.loop(0, HEADS + LAG_SUMS)
    def _(i):
        @pl.when(jnp.logical_and(earlier, i < HEADS - AHEAD))
        def _():
            qg_copy(i + AHEAD).start()

        @pl.when(i < HEADS)
        def _():
            scores(i)

        @pl.when(jnp.logical_and(i >= LAG_GRADS, i < HEADS + LAG_GRADS))
        def _():
            grads(i - LAG_GRADS)

        @pl.when(i >= LAG_SUMS)
        def _():
            sums(i - LAG_SUMS)

    @pl.when(earlier)
    def _():
        gate_copy().wait_send()

    @pl.loop(0, HEADS)
    def _(h):
        @pl.when(earlier)
        def _():
            qg_copy(h).wait_send()
            stat_copy(h, 0).wait_send()

        @pl.when(later)
        def _():
            stat_copy(h, 1).wait_send()
            dq_copy(h).wait_send()

        for side, (there, _) in enumerate(sides):
            @pl.when(there)
            def _(side=side):
                kv_copy(h, side).wait_send()
                dkv_copy(h, side).wait_send()


def store(dq, dk, dv, dq_out, dk_out, dv_out, sem):
    copies = [
        pltpu.make_async_copy(src, dst, sem.at[k])
        for k, (src, dst) in enumerate(((dq, dq_out), (dk, dk_out), (dv, dv_out)))
    ]
    for c in copies:
        c.start()
    for c in copies:
        c.wait()


def solution(mesh):
    frames, blocks = mesh.shape["tm"], mesh.shape["seq"]

    def body(queries, keys, values, grad_out, block_mask, valid_len):
        _, n, feat = queries.shape
        hd = feat // HEADS
        out = jax.ShapeDtypeStruct(queries.shape, queries.dtype)
        vmem = pl.BlockSpec(memory_space=pltpu.VMEM)
        smem = pl.BlockSpec(memory_space=pltpu.SMEM)
        hbm = pl.BlockSpec(memory_space=pl.ANY)
        dma = pltpu.SemaphoreType.DMA
        held = pltpu.VMEM(queries.shape, queries.dtype)
        grads = pl.pallas_call(
            functools.partial(kernel, frames, blocks, n, hd),
            out_shape=(held,) * 3,
            in_specs=[hbm] * 4 + [smem] * 2,
            out_specs=(vmem,) * 3,
            scratch_shapes=[
                pltpu.VMEM((2, 3 * n, feat), jnp.bfloat16),
                pltpu.VMEM((2, 2 * n, feat), jnp.bfloat16),
                pltpu.VMEM((3 * n, 2 * n), jnp.float32),
                pltpu.VMEM((2, 8, n), jnp.float32),
                pltpu.VMEM((RING, 3 * n, 2 * n), jnp.float32),
                pltpu.VMEM((RING, 3 * n, 2 * n), jnp.float32),
                pltpu.VMEM((HEADS, 8, 2 * n), jnp.float32),
                pltpu.VMEM((HEADS, 8, 2 * n), jnp.float32),
                pltpu.VMEM((n, feat), jnp.float32),
                pltpu.VMEM((n, feat), jnp.float32),
                pltpu.VMEM((n, feat), jnp.float32),
                pltpu.VMEM((HEADS, n, hd), jnp.bfloat16),
                pltpu.VMEM((HEADS, n, hd), jnp.bfloat16),
                pltpu.VMEM((2, HEADS, 2 * n, hd), jnp.bfloat16),
                pltpu.VMEM((2, HEADS, 2 * n, hd), jnp.bfloat16),
                dma((4,)),
                dma((2, HEADS)),
                dma((2, HEADS)),
                dma((HEADS,)),
                dma((HEADS,)),
                dma((2,)),
                dma((2, HEADS)),
                dma((2, HEADS)),
                dma((HEADS,)),
                dma((HEADS,)),
                dma((2, HEADS)),
                dma((2, HEADS)),
            ],
            compiler_params=pltpu.CompilerParams(collective_id=0, has_side_effects=True),
        )(keys, values, queries, grad_out, block_mask, valid_len)
        return pl.pallas_call(
            store,
            out_shape=(out,) * 3,
            in_specs=[vmem] * 3,
            out_specs=(hbm,) * 3,
            scratch_shapes=[dma((3,))],
        )(*(pltpu.with_memory_space_constraint(x, pltpu.VMEM) for x in grads))

    spec = P("tm", "seq", None)
    return jax.shard_map(
        body, mesh=mesh, in_specs=(spec,) * 5 + (P(),), out_specs=(spec,) * 3, check_vma=False
    )
```

```python
import functools
import math

import jax
import jax.numpy as jnp
from jax import lax
from jax.experimental import pallas as pl
from jax.experimental.pallas import tpu as pltpu
from jax.sharding import PartitionSpec as P

HEADS = 8
AHEAD = 4
LEAD_OWN = 2
LAG_GRADS = 3
LAG_SUMS = 6
BIG = 1e30
MESH = pl.DeviceIdType.MESH
NT = (((1,), (1,)), ((), ()))
TN = (((0,), (0,)), ((), ()))
NN = (((1,), (0,)), ((), ()))


def dot(a, b, dims):
    return lax.dot_general(a, b, dims, preferred_element_type=jnp.float32)


def kernel(
    frames, blocks, block_len, head_dim,
    k_in, v_in, q_in, g_in, mask_in, valid_in,
    dq_ref, dk_ref, dv_ref,
    kv, qg, bias, gate, e_all, d_all, stat, stat_far, dq_home, dk_home, dv_home,
    dq_out, dq_far, dkv_out, dkv_far,
    mask_ref, valid_ref, own_sem, kv_send, kv_recv, qg_send, qg_recv, gate_sem, stat_send, stat_recv, dq_send, dq_recv, dkv_send, dkv_recv,
):
    n = block_len
    t = lax.axis_index("tm")
    s = lax.axis_index("seq")
    scale = head_dim ** (-0.5)
    scale2 = scale * math.log2(math.e)
    left, right = s > 0, s < blocks - 1
    earlier, later = t > 0, t < frames - 1
    sides = ((left, -1), (right, 1))

    def cols(h):
        return pl.ds(pl.multiple_of(h * head_dim, head_dim), head_dim)

    def remote(src, dst, send, recv, dt, ds):
        return pltpu.make_async_remote_copy(
            src_ref=src, dst_ref=dst, send_sem=send, recv_sem=recv,
            device_id=(t + dt, s + ds), device_id_type=MESH,
        )

    def kv_copy(h, side):
        slot = 2 - 2 * side
        return remote(
            kv.at[:, n:2 * n, cols(h)], kv.at[:, slot * n:(slot + 1) * n, cols(h)],
            kv_send.at[side, h], kv_recv.at[side, h], 0, (-1, 1)[side],
        )

    def qg_copy(h):
        return remote(qg.at[:, :n, cols(h)], qg.at[:, n:, cols(h)], qg_send.at[h], qg_recv.at[h], -1, 0)

    def gate_copy():
        return remote(gate.at[0], gate.at[1], gate_sem.at[0], gate_sem.at[1], -1, 0)

    def stat_copy(h, up):
        src, dst = ((slice(0, n), slice(n, 2 * n)), (slice(n, 2 * n), slice(0, n)))[up]
        return remote(
            stat.at[h, :, src], stat_far.at[h, :, dst], stat_send.at[up, h], stat_recv.at[up, h], (-1, 1)[up], 0
        )

    def dq_copy(h):
        return remote(dq_out.at[h], dq_far.at[h], dq_send.at[h], dq_recv.at[h], 1, 0)

    def dkv_copy(h, side):
        return remote(
            dkv_out.at[side, h], dkv_far.at[side, h], dkv_send.at[side, h], dkv_recv.at[side, h], 0, (-1, 1)[side]
        )

    barrier = pltpu.get_barrier_semaphore()
    expected = jnp.int32(0)
    for there, dt, ds in ((left, 0, -1), (right, 0, 1), (earlier, -1, 0), (later, 1, 0)):
        expected = expected + there.astype(jnp.int32)

        @pl.when(there)
        def _(dt=dt, ds=ds):
            pl.semaphore_signal(barrier, inc=1, device_id=(t + dt, s + ds), device_id_type=MESH)

    own = [
        pltpu.make_async_copy(k_in.at[0], kv.at[0, n:2 * n], own_sem.at[0]),
        pltpu.make_async_copy(v_in.at[0], kv.at[1, n:2 * n], own_sem.at[1]),
        pltpu.make_async_copy(q_in.at[0], qg.at[0, :n], own_sem.at[2]),
        pltpu.make_async_copy(g_in.at[0], qg.at[1, :n], own_sem.at[3]),
    ]
    small = [
        pltpu.make_async_copy(mask_in, mask_ref, own_sem.at[4]),
        pltpu.make_async_copy(valid_in, valid_ref, own_sem.at[5]),
    ]
    for c in small + own:
        c.start()
    for c in small:
        c.wait()

    for c in range(3):
        gate[0, c:c + 1, :] = jnp.full((1, n), jnp.where(mask_ref[0, 0, 3 + c] == 1, 1.0, 0.0), jnp.float32)

    for c in own:
        c.wait()
    pl.semaphore_wait(barrier, expected)

    @pl.when(earlier)
    def _():
        gate_copy().start()

    @pl.loop(0, HEADS)
    def _(h):
        @pl.when(jnp.logical_and(earlier, h < AHEAD))
        def _():
            qg_copy(h).start()

        for side, (there, _) in enumerate(sides):
            @pl.when(there)
            def _(side=side):
                kv_copy(h, side).start()

    row = lax.broadcasted_iota(jnp.int32, (n, n), 0)
    frame_valid = valid_ref[t]

    def key_limit(c):
        near = s + c - 1
        inside = jnp.logical_and(near >= 0, near < blocks).astype(jnp.int32)
        return jnp.maximum(frame_valid - near * n, 0) * inside

    for c in range(3):
        limit = key_limit(c) * jnp.where(mask_ref[0, 0, c] == 1, 1, 0)
        bias[c * n:(c + 1) * n, :n] = jnp.where(row < limit, 0.0, -BIG)

    lane = lax.broadcasted_iota(jnp.int32, (1, 2 * n), 1)
    next_valid = valid_ref[jnp.minimum(t + 1, frames - 1)] * later.astype(jnp.int32)
    okay = jnp.where(lane < jnp.where(lane < n, jnp.minimum(frame_valid - s * n, n), next_valid - s * n + n), 1.0, 0.0)

    zeros = jnp.zeros((n, kv.shape[2]), kv.dtype)
    none = jnp.where(lax.broadcasted_iota(jnp.int32, (8, n), 0) == 0, -BIG, 0.0)
    for slot, there in ((0, left), (2, right)):
        @pl.when(jnp.logical_not(there))
        def _(slot=slot):
            for k in range(2):
                kv[k, slot * n:(slot + 1) * n, :] = zeros
            dkv_far[1 - slot // 2] = jnp.zeros(dkv_far.shape[1:], dkv_far.dtype)

    @pl.when(jnp.logical_not(later))
    def _():
        for k in range(2):
            qg[k, n:, :] = zeros
        gate[1] = jnp.zeros((8, n), jnp.float32)
        for h in range(HEADS):
            stat_far[h, :, n:] = none
            stat[h, :, n:] = jnp.ones((8, n), jnp.float32)
            e_all[h, :, n:] = jnp.zeros((3 * n, n), jnp.float32)
            d_all[h, :, n:] = jnp.zeros((3 * n, n), jnp.float32)

    @pl.when(jnp.logical_not(earlier))
    def _():
        dq_far[...] = jnp.zeros(dq_far.shape, dq_far.dtype)
        for h in range(HEADS):
            stat_far[h, :, :n] = none

    @pl.when(later)
    def _():
        gate_copy().wait_recv()

    for c in range(3):
        open_here = jnp.logical_and(row < key_limit(c), gate[1, c:c + 1, :] > 0.5)
        bias[c * n:(c + 1) * n, n:] = jnp.where(open_here, 0.0, -BIG)

    def scores(h, half):
        hc = cols(h)
        q = slice(half * n, (half + 1) * n)
        score = dot(kv[0, :, hc], qg[0, q, hc], NT) * scale2 + bias[:, q]
        peak = jnp.max(score, axis=0, keepdims=True)
        e = jnp.exp2(score - peak)
        dprob = dot(kv[1, :, hc], qg[1, q, hc], NT)
        e_all[h, :, q] = e
        d_all[h, :, q] = dprob
        stat[h, 0:1, q] = peak
        stat[h, 1:2, q] = jnp.sum(e, axis=0, keepdims=True)
        stat[h, 2:3, q] = jnp.sum(e * dprob, axis=0, keepdims=True)

    def own_scores(h):
        for side, (there, _) in enumerate(sides):
            @pl.when(there)
            def _(side=side):
                kv_copy(h, 1 - side).wait_recv()

        scores(h, 0)

        @pl.when(earlier)
        def _():
            stat_copy(h, 0).start()

    def next_scores(h):
        @pl.when(later)
        def _():
            qg_copy(h).wait_recv()
            scores(h, 1)
            stat_copy(h, 1).start()

    def grads(h):
        @pl.when(earlier)
        def _():
            stat_copy(h, 1).wait_recv()

        @pl.when(later)
        def _():
            stat_copy(h, 0).wait_recv()

        hc = cols(h)
        near, far = stat[h], stat_far[h]
        peak = jnp.maximum(near[0:1], far[0:1])
        a, b = jnp.exp2(near[0:1] - peak), jnp.exp2(far[0:1] - peak)
        norm = 1.0 / (near[1:2] * a + far[1:2] * b)
        row_dot = (near[2:3] * a + far[2:3] * b) * norm
        prob = e_all[h] * (okay * a * norm)
        dscore = (prob * (d_all[h] - row_dot)).astype(jnp.bfloat16)
        query, grad, key = qg[0, :, hc], qg[1, :, hc], kv[0, :, hc]
        dq = dot(dscore, key, TN) * scale
        dq_home[:, hc] = dq[:n]
        dq_out[h] = dq[n:].astype(dq_out.dtype)

        @pl.when(later)
        def _():
            dq_copy(h).start()

        dk = dot(dscore, query, NN) * scale
        dv = dot(prob.astype(jnp.bfloat16), grad, NN)
        dk_home[:, hc] = dk[n:2 * n]
        dv_home[:, hc] = dv[n:2 * n]
        for side, (there, _) in enumerate(sides):
            part = slice(2 * side * n, (2 * side + 1) * n)
            dkv_out[side, h, :n] = dk[part].astype(dkv_out.dtype)
            dkv_out[side, h, n:] = dv[part].astype(dkv_out.dtype)

            @pl.when(there)
            def _(side=side):
                dkv_copy(h, side).start()

    def sums(h):
        hc = cols(h)

        @pl.when(earlier)
        def _():
            dq_copy(h).wait_recv()

        dq_ref[0, :, hc] = (dq_home[:, hc] + dq_far[h].astype(jnp.float32)).astype(dq_ref.dtype)
        for side, (there, _) in enumerate(sides):
            @pl.when(there)
            def _(side=side):
                dkv_copy(h, 1 - side).wait_recv()
        from_right, from_left = dkv_far[0, h].astype(jnp.float32), dkv_far[1, h].astype(jnp.float32)
        both = from_right + from_left
        dk_ref[0, :, hc] = (dk_home[:, hc] + both[:n]).astype(dk_ref.dtype)
        dv_ref[0, :, hc] = (dv_home[:, hc] + both[n:]).astype(dv_ref.dtype)

    @pl.loop(0, LEAD_OWN)
    def _(h):
        own_scores(h)

    @pl.loop(0, HEADS + LAG_SUMS)
    def _(i):
        @pl.when(i < HEADS)
        def _():
            next_scores(i)

        @pl.when(jnp.logical_and(earlier, i < HEADS - AHEAD))
        def _():
            qg_copy(i + AHEAD).start()

        @pl.when(jnp.logical_and(i >= LAG_GRADS, i < HEADS + LAG_GRADS))
        def _():
            grads(i - LAG_GRADS)

        @pl.when(i < HEADS - LEAD_OWN)
        def _():
            own_scores(i + LEAD_OWN)

        @pl.when(i >= LAG_SUMS)
        def _():
            sums(i - LAG_SUMS)

    @pl.when(earlier)
    def _():
        gate_copy().wait_send()

    @pl.loop(0, HEADS)
    def _(h):
        @pl.when(earlier)
        def _():
            qg_copy(h).wait_send()
            stat_copy(h, 0).wait_send()

        @pl.when(later)
        def _():
            stat_copy(h, 1).wait_send()
            dq_copy(h).wait_send()

        for side, (there, _) in enumerate(sides):
            @pl.when(there)
            def _(side=side):
                kv_copy(h, side).wait_send()
                dkv_copy(h, side).wait_send()


def store(dq, dk, dv, dq_out, dk_out, dv_out, sem):
    copies = [
        pltpu.make_async_copy(src, dst, sem.at[k])
        for k, (src, dst) in enumerate(((dq, dq_out), (dk, dk_out), (dv, dv_out)))
    ]
    for c in copies:
        c.start()
    for c in copies:
        c.wait()


def solution(mesh):
    frames, blocks = mesh.shape["tm"], mesh.shape["seq"]

    def body(queries, keys, values, grad_out, block_mask, valid_len):
        _, n, feat = queries.shape
        hd = feat // HEADS
        out = jax.ShapeDtypeStruct(queries.shape, queries.dtype)
        vmem = pl.BlockSpec(memory_space=pltpu.VMEM)
        hbm = pl.BlockSpec(memory_space=pl.ANY)
        dma = pltpu.SemaphoreType.DMA
        held = pltpu.VMEM(queries.shape, queries.dtype)
        grads = pl.pallas_call(
            functools.partial(kernel, frames, blocks, n, hd),
            out_shape=(held,) * 3,
            in_specs=[hbm] * 6,
            out_specs=(vmem,) * 3,
            scratch_shapes=[
                pltpu.VMEM((2, 3 * n, feat), jnp.bfloat16),
                pltpu.VMEM((2, 2 * n, feat), jnp.bfloat16),
                pltpu.VMEM((3 * n, 2 * n), jnp.float32),
                pltpu.VMEM((2, 8, n), jnp.float32),
                pltpu.VMEM((HEADS, 3 * n, 2 * n), jnp.float32),
                pltpu.VMEM((HEADS, 3 * n, 2 * n), jnp.float32),
                pltpu.VMEM((HEADS, 8, 2 * n), jnp.float32),
                pltpu.VMEM((HEADS, 8, 2 * n), jnp.float32),
                pltpu.VMEM((n, feat), jnp.float32),
                pltpu.VMEM((n, feat), jnp.float32),
                pltpu.VMEM((n, feat), jnp.float32),
                pltpu.VMEM((HEADS, n, hd), jnp.bfloat16),
                pltpu.VMEM((HEADS, n, hd), jnp.bfloat16),
                pltpu.VMEM((2, HEADS, 2 * n, hd), jnp.bfloat16),
                pltpu.VMEM((2, HEADS, 2 * n, hd), jnp.bfloat16),
                pltpu.SMEM(block_mask.shape, jnp.int32),
                pltpu.SMEM(valid_len.shape, jnp.int32),
                dma((6,)),
                dma((2, HEADS)),
                dma((2, HEADS)),
                dma((HEADS,)),
                dma((HEADS,)),
                dma((2,)),
                dma((2, HEADS)),
                dma((2, HEADS)),
                dma((HEADS,)),
                dma((HEADS,)),
                dma((2, HEADS)),
                dma((2, HEADS)),
            ],
            compiler_params=pltpu.CompilerParams(collective_id=0, has_side_effects=True),
        )(keys, values, queries, grad_out, block_mask, valid_len)
        return pl.pallas_call(
            store,
            out_shape=(out,) * 3,
            in_specs=[vmem] * 3,
            out_specs=(hbm,) * 3,
            scratch_shapes=[dma((3,))],
        )(*(pltpu.with_memory_space_constraint(x, pltpu.VMEM) for x in grads))

    spec = P("tm", "seq", None)
    return jax.shard_map(
        body, mesh=mesh, in_specs=(spec,) * 5 + (P(),), out_specs=(spec,) * 3, check_vma=False
    )
```

```python
import functools
import math

import jax
import jax.numpy as jnp
from jax import lax
from jax.experimental import pallas as pl
from jax.experimental.pallas import tpu as pltpu
from jax.sharding import PartitionSpec as P

HEADS = 8
AHEAD = 4
LEAD_OWN = 2
LAG_GRADS = 3
LAG_SUMS = 10
BIG = 1e30
MESH = pl.DeviceIdType.MESH
NT = (((1,), (1,)), ((), ()))
TN = (((0,), (0,)), ((), ()))
NN = (((1,), (0,)), ((), ()))


def dot(a, b, dims):
    return lax.dot_general(a, b, dims, preferred_element_type=jnp.float32)


def kernel(
    frames, blocks, block_len, head_dim,
    k_in, v_in, q_in, g_in, mask_in, valid_in,
    dq_ref, dk_ref, dv_ref,
    kv, qg, bias, gate, e_all, d_all, stat, stat_far, dq_home, dk_home, dv_home,
    dq_out, dq_far, dkv_out, dkv_far,
    mask_ref, valid_ref, own_sem, kv_send, kv_recv, qg_send, qg_recv, gate_sem, stat_send, stat_recv, dq_send, dq_recv, dkv_send, dkv_recv,
):
    n = block_len
    t = lax.axis_index("tm")
    s = lax.axis_index("seq")
    scale = head_dim ** (-0.5)
    scale2 = scale * math.log2(math.e)
    left, right = s > 0, s < blocks - 1
    earlier, later = t > 0, t < frames - 1
    sides = ((left, -1), (right, 1))

    def cols(h):
        return pl.ds(pl.multiple_of(h * head_dim, head_dim), head_dim)

    def remote(src, dst, send, recv, dt, ds):
        return pltpu.make_async_remote_copy(
            src_ref=src, dst_ref=dst, send_sem=send, recv_sem=recv,
            device_id=(t + dt, s + ds), device_id_type=MESH,
        )

    def kv_copy(h, side):
        slot = 2 - 2 * side
        return remote(
            kv.at[:, n:2 * n, cols(h)], kv.at[:, slot * n:(slot + 1) * n, cols(h)],
            kv_send.at[side, h], kv_recv.at[side, h], 0, (-1, 1)[side],
        )

    def qg_copy(h):
        return remote(qg.at[:, :n, cols(h)], qg.at[:, n:, cols(h)], qg_send.at[h], qg_recv.at[h], -1, 0)

    def gate_copy():
        return remote(gate.at[0], gate.at[1], gate_sem.at[0], gate_sem.at[1], -1, 0)

    def stat_copy(h, up):
        src, dst = ((slice(0, n), slice(n, 2 * n)), (slice(n, 2 * n), slice(0, n)))[up]
        return remote(
            stat.at[h, :, src], stat_far.at[h, :, dst], stat_send.at[up, h], stat_recv.at[up, h], (-1, 1)[up], 0
        )

    def dq_copy(h):
        return remote(dq_out.at[h], dq_far.at[h], dq_send.at[h], dq_recv.at[h], 1, 0)

    def dkv_copy(h, side):
        return remote(
            dkv_out.at[side, h], dkv_far.at[side, h], dkv_send.at[side, h], dkv_recv.at[side, h], 0, (-1, 1)[side]
        )

    barrier = pltpu.get_barrier_semaphore()
    expected = jnp.int32(0)
    for there, dt, ds in ((left, 0, -1), (right, 0, 1), (earlier, -1, 0), (later, 1, 0)):
        expected = expected + there.astype(jnp.int32)

        @pl.when(there)
        def _(dt=dt, ds=ds):
            pl.semaphore_signal(barrier, inc=1, device_id=(t + dt, s + ds), device_id_type=MESH)

    own = [
        pltpu.make_async_copy(k_in.at[0], kv.at[0, n:2 * n], own_sem.at[0]),
        pltpu.make_async_copy(v_in.at[0], kv.at[1, n:2 * n], own_sem.at[1]),
        pltpu.make_async_copy(q_in.at[0], qg.at[0, :n], own_sem.at[2]),
        pltpu.make_async_copy(g_in.at[0], qg.at[1, :n], own_sem.at[3]),
    ]
    small = [
        pltpu.make_async_copy(mask_in, mask_ref, own_sem.at[4]),
        pltpu.make_async_copy(valid_in, valid_ref, own_sem.at[5]),
    ]
    for c in small + own:
        c.start()
    for c in small:
        c.wait()

    for c in range(3):
        gate[0, c:c + 1, :] = jnp.full((1, n), jnp.where(mask_ref[0, 0, 3 + c] == 1, 1.0, 0.0), jnp.float32)

    for c in own:
        c.wait()
    pl.semaphore_wait(barrier, expected)

    @pl.when(earlier)
    def _():
        gate_copy().start()

    @pl.loop(0, HEADS)
    def _(h):
        @pl.when(jnp.logical_and(earlier, h < AHEAD))
        def _():
            qg_copy(h).start()

        for side, (there, _) in enumerate(sides):
            @pl.when(there)
            def _(side=side):
                kv_copy(h, side).start()

    row = lax.broadcasted_iota(jnp.int32, (n, n), 0)
    frame_valid = valid_ref[t]

    def key_limit(c):
        near = s + c - 1
        inside = jnp.logical_and(near >= 0, near < blocks).astype(jnp.int32)
        return jnp.maximum(frame_valid - near * n, 0) * inside

    for c in range(3):
        limit = key_limit(c) * jnp.where(mask_ref[0, 0, c] == 1, 1, 0)
        bias[c * n:(c + 1) * n, :n] = jnp.where(row < limit, 0.0, -BIG)

    lane = lax.broadcasted_iota(jnp.int32, (1, 2 * n), 1)
    next_valid = valid_ref[jnp.minimum(t + 1, frames - 1)] * later.astype(jnp.int32)
    okay = jnp.where(lane < jnp.where(lane < n, jnp.minimum(frame_valid - s * n, n), next_valid - s * n + n), 1.0, 0.0)

    zeros = jnp.zeros((n, kv.shape[2]), kv.dtype)
    none = jnp.where(lax.broadcasted_iota(jnp.int32, (4, n), 0) == 0, -BIG, 0.0)
    for slot, there in ((0, left), (2, right)):
        @pl.when(jnp.logical_not(there))
        def _(slot=slot):
            for k in range(2):
                kv[k, slot * n:(slot + 1) * n, :] = zeros
            dkv_far[1 - slot // 2] = jnp.zeros(dkv_far.shape[1:], dkv_far.dtype)

    @pl.when(jnp.logical_not(later))
    def _():
        for k in range(2):
            qg[k, n:, :] = zeros
        gate[1] = jnp.zeros((4, n), jnp.float32)
        for h in range(HEADS):
            stat_far[h, :, n:] = none
            stat[h, :, n:] = jnp.ones((4, n), jnp.float32)
            e_all[h, :, n:] = jnp.zeros((3 * n, n), jnp.float32)
            d_all[h, :, n:] = jnp.zeros((3 * n, n), jnp.float32)

    @pl.when(jnp.logical_not(earlier))
    def _():
        dq_far[...] = jnp.zeros(dq_far.shape, dq_far.dtype)
        for h in range(HEADS):
            stat_far[h, :, :n] = none

    @pl.when(later)
    def _():
        gate_copy().wait_recv()

    for c in range(3):
        open_here = jnp.logical_and(row < key_limit(c), gate[1, c:c + 1, :] > 0.5)
        bias[c * n:(c + 1) * n, n:] = jnp.where(open_here, 0.0, -BIG)

    def scores(h, half):
        hc = cols(h)
        q = slice(half * n, (half + 1) * n)
        score = dot(kv[0, :, hc], qg[0, q, hc], NT) * scale2 + bias[:, q]
        peak = jnp.max(score, axis=0, keepdims=True)
        e = jnp.exp2(score - peak)
        dprob = dot(kv[1, :, hc], qg[1, q, hc], NT)
        e_all[h, :, q] = e
        d_all[h, :, q] = dprob
        stat[h, 0:1, q] = peak
        stat[h, 1:2, q] = jnp.sum(e, axis=0, keepdims=True)
        stat[h, 2:3, q] = jnp.sum(e * dprob, axis=0, keepdims=True)

    def own_scores(h):
        for side, (there, _) in enumerate(sides):
            @pl.when(there)
            def _(side=side):
                kv_copy(h, 1 - side).wait_recv()

        scores(h, 0)

        @pl.when(earlier)
        def _():
            stat_copy(h, 0).start()

    def next_scores(h):
        @pl.when(later)
        def _():
            qg_copy(h).wait_recv()
            scores(h, 1)
            stat_copy(h, 1).start()

    def grads(h):
        @pl.when(earlier)
        def _():
            stat_copy(h, 1).wait_recv()

        @pl.when(later)
        def _():
            stat_copy(h, 0).wait_recv()

        hc = cols(h)
        near, far = stat[h], stat_far[h]
        peak = jnp.maximum(near[0:1], far[0:1])
        a, b = jnp.exp2(near[0:1] - peak), jnp.exp2(far[0:1] - peak)
        norm = 1.0 / (near[1:2] * a + far[1:2] * b)
        row_dot = (near[2:3] * a + far[2:3] * b) * norm
        prob = e_all[h] * (okay * a * norm)
        dscore = (prob * (d_all[h] - row_dot)).astype(jnp.bfloat16)
        query, grad, key = qg[0, :, hc], qg[1, :, hc], kv[0, :, hc]
        dk = dot(dscore, query, NN) * scale
        dv = dot(prob.astype(jnp.bfloat16), grad, NN)
        dk_home[:, hc] = dk[n:2 * n]
        dv_home[:, hc] = dv[n:2 * n]
        for side, (there, _) in enumerate(sides):
            part = slice(2 * side * n, (2 * side + 1) * n)
            dkv_out[side, h, :n] = dk[part].astype(dkv_out.dtype)
            dkv_out[side, h, n:] = dv[part].astype(dkv_out.dtype)

            @pl.when(there)
            def _(side=side):
                dkv_copy(h, side).start()

        dq = dot(dscore, key, TN) * scale
        dq_home[:, hc] = dq[:n]
        dq_out[h] = dq[n:].astype(dq_out.dtype)

        @pl.when(later)
        def _():
            dq_copy(h).start()

    def sums(h):
        hc = cols(h)

        @pl.when(earlier)
        def _():
            dq_copy(h).wait_recv()

        dq_ref[0, :, hc] = (dq_home[:, hc] + dq_far[h].astype(jnp.float32)).astype(dq_ref.dtype)
        for side, (there, _) in enumerate(sides):
            @pl.when(there)
            def _(side=side):
                dkv_copy(h, 1 - side).wait_recv()
        from_right, from_left = dkv_far[0, h].astype(jnp.float32), dkv_far[1, h].astype(jnp.float32)
        both = from_right + from_left
        dk_ref[0, :, hc] = (dk_home[:, hc] + both[:n]).astype(dk_ref.dtype)
        dv_ref[0, :, hc] = (dv_home[:, hc] + both[n:]).astype(dv_ref.dtype)

    def inputs_sent(h):
        @pl.when(earlier)
        def _():
            qg_copy(h).wait_send()

        for side, (there, _) in enumerate(sides):
            @pl.when(there)
            def _(side=side):
                kv_copy(h, side).wait_send()

    def totals_sent(h):
        @pl.when(earlier)
        def _():
            stat_copy(h, 0).wait_send()

        @pl.when(later)
        def _():
            stat_copy(h, 1).wait_send()

    def grads_sent(h):
        @pl.when(later)
        def _():
            dq_copy(h).wait_send()

        for side, (there, _) in enumerate(sides):
            @pl.when(there)
            def _(side=side):
                dkv_copy(h, side).wait_send()

    @pl.loop(0, LEAD_OWN)
    def _(h):
        own_scores(h)

    @pl.loop(0, HEADS + LAG_SUMS)
    def _(i):
        @pl.when(i < HEADS)
        def _():
            next_scores(i)

        @pl.when(jnp.logical_and(earlier, i < HEADS - AHEAD))
        def _():
            qg_copy(i + AHEAD).start()

        @pl.when(jnp.logical_and(i >= LAG_GRADS, i < HEADS + LAG_GRADS))
        def _():
            grads(i - LAG_GRADS)

        @pl.when(i < HEADS - LEAD_OWN)
        def _():
            own_scores(i + LEAD_OWN)

        @pl.when(i == HEADS + 1)
        def _():
            @pl.when(earlier)
            def _():
                gate_copy().wait_send()

            @pl.loop(0, HEADS)
            def _(h):
                inputs_sent(h)

        @pl.when(i == HEADS + 2)
        def _():
            @pl.loop(0, HEADS)
            def _(h):
                totals_sent(h)

        @pl.when(i >= LAG_SUMS)
        def _():
            sums(i - LAG_SUMS)
            grads_sent(i - LAG_SUMS)


def store(dq, dk, dv, dq_out, dk_out, dv_out, sem):
    copies = [
        pltpu.make_async_copy(src, dst, sem.at[k])
        for k, (src, dst) in enumerate(((dq, dq_out), (dk, dk_out), (dv, dv_out)))
    ]
    for c in copies:
        c.start()
    for c in copies:
        c.wait()


def solution(mesh):
    frames, blocks = mesh.shape["tm"], mesh.shape["seq"]

    def body(queries, keys, values, grad_out, block_mask, valid_len):
        _, n, feat = queries.shape
        hd = feat // HEADS
        out = jax.ShapeDtypeStruct(queries.shape, queries.dtype)
        vmem = pl.BlockSpec(memory_space=pltpu.VMEM)
        hbm = pl.BlockSpec(memory_space=pl.ANY)
        dma = pltpu.SemaphoreType.DMA
        held = pltpu.VMEM(queries.shape, queries.dtype)
        grads = pl.pallas_call(
            functools.partial(kernel, frames, blocks, n, hd),
            out_shape=(held,) * 3,
            in_specs=[hbm] * 6,
            out_specs=(vmem,) * 3,
            scratch_shapes=[
                pltpu.VMEM((2, 3 * n, feat), jnp.bfloat16),
                pltpu.VMEM((2, 2 * n, feat), jnp.bfloat16),
                pltpu.VMEM((3 * n, 2 * n), jnp.float32),
                pltpu.VMEM((2, 4, n), jnp.float32),
                pltpu.VMEM((HEADS, 3 * n, 2 * n), jnp.float32),
                pltpu.VMEM((HEADS, 3 * n, 2 * n), jnp.float32),
                pltpu.VMEM((HEADS, 4, 2 * n), jnp.float32),
                pltpu.VMEM((HEADS, 4, 2 * n), jnp.float32),
                pltpu.VMEM((n, feat), jnp.float32),
                pltpu.VMEM((n, feat), jnp.float32),
                pltpu.VMEM((n, feat), jnp.float32),
                pltpu.VMEM((HEADS, n, hd), jnp.bfloat16),
                pltpu.VMEM((HEADS, n, hd), jnp.bfloat16),
                pltpu.VMEM((2, HEADS, 2 * n, hd), jnp.bfloat16),
                pltpu.VMEM((2, HEADS, 2 * n, hd), jnp.bfloat16),
                pltpu.SMEM(block_mask.shape, jnp.int32),
                pltpu.SMEM(valid_len.shape, jnp.int32),
                dma((6,)),
                dma((2, HEADS)),
                dma((2, HEADS)),
                dma((HEADS,)),
                dma((HEADS,)),
                dma((2,)),
                dma((2, HEADS)),
                dma((2, HEADS)),
                dma((HEADS,)),
                dma((HEADS,)),
                dma((2, HEADS)),
                dma((2, HEADS)),
            ],
            compiler_params=pltpu.CompilerParams(collective_id=0, has_side_effects=True),
        )(keys, values, queries, grad_out, block_mask, valid_len)
        return pl.pallas_call(
            store,
            out_shape=(out,) * 3,
            in_specs=[vmem] * 3,
            out_specs=(hbm,) * 3,
            scratch_shapes=[dma((3,))],
        )(*(pltpu.with_memory_space_constraint(x, pltpu.VMEM) for x in grads))

    spec = P("tm", "seq", None)
    return jax.shard_map(
        body, mesh=mesh, in_specs=(spec,) * 5 + (P(),), out_specs=(spec,) * 3, check_vma=False
    )
```

```python
import functools
import math

import jax
import jax.numpy as jnp
from jax import lax
from jax.experimental import pallas as pl
from jax.experimental.pallas import tpu as pltpu
from jax.sharding import PartitionSpec as P

HEADS = 8
AHEAD = 4
HELD = 2
HELD_LAST = 3
LEAD_OWN = 3
LAG_GRADS = 3
LAG_FIRST = 2
LAG_SUMS = 10
BIG = 1e30
MESH = pl.DeviceIdType.MESH
NT = (((1,), (1,)), ((), ()))
TN = (((0,), (0,)), ((), ()))
NN = (((1,), (0,)), ((), ()))


def dot(a, b, dims):
    return lax.dot_general(a, b, dims, preferred_element_type=jnp.float32)


def kernel(
    frames, blocks, block_len, head_dim,
    k_in, v_in, q_in, g_in, mask_in, valid_in,
    dq_ref, dk_ref, dv_ref,
    kv, qg, bias, gate, e_all, d_all, stat, stat_far, dq_home, dk_home, dv_home,
    dq_out, dq_far, dkv_out, dkv_far,
    mask_ref, valid_ref, own_sem, kv_send, kv_recv, qg_send, qg_recv, gate_sem, stat_send, stat_recv, dq_send, dq_recv, dkv_send, dkv_recv,
):
    n = block_len
    t = lax.axis_index("tm")
    s = lax.axis_index("seq")
    scale = head_dim ** (-0.5)
    scale2 = scale * math.log2(math.e)
    left, right = s > 0, s < blocks - 1
    earlier, later = t > 0, t < frames - 1
    sides = ((left, -1), (right, 1))

    def cols(h):
        return pl.ds(pl.multiple_of(h * head_dim, head_dim), head_dim)

    def remote(src, dst, send, recv, dt, ds):
        return pltpu.make_async_remote_copy(
            src_ref=src, dst_ref=dst, send_sem=send, recv_sem=recv,
            device_id=(t + dt, s + ds), device_id_type=MESH,
        )

    def kv_copy(h, side):
        slot = 2 - 2 * side
        return remote(
            kv.at[:, n:2 * n, cols(h)], kv.at[:, slot * n:(slot + 1) * n, cols(h)],
            kv_send.at[side, h], kv_recv.at[side, h], 0, (-1, 1)[side],
        )

    def qg_copy(h):
        return remote(qg.at[:, :n, cols(h)], qg.at[:, n:, cols(h)], qg_send.at[h], qg_recv.at[h], -1, 0)

    def gate_copy():
        return remote(gate.at[0], gate.at[1], gate_sem.at[0], gate_sem.at[1], -1, 0)

    def stat_copy(h, up):
        src, dst = ((slice(0, n), slice(n, 2 * n)), (slice(n, 2 * n), slice(0, n)))[up]
        return remote(
            stat.at[h, :, src], stat_far.at[h, :, dst], stat_send.at[up, h], stat_recv.at[up, h], (-1, 1)[up], 0
        )

    def dq_copy(h):
        return remote(dq_out.at[h], dq_far.at[h], dq_send.at[h], dq_recv.at[h], 1, 0)

    def dkv_copy(h, side):
        return remote(
            dkv_out.at[side, h], dkv_far.at[side, h], dkv_send.at[side, h], dkv_recv.at[side, h], 0, (-1, 1)[side]
        )

    def dkv_half(h, side, k):
        rows = slice(k * n, (k + 1) * n)
        return remote(
            dkv_out.at[side, h, rows], dkv_far.at[side, h, rows],
            dkv_send.at[side, h], dkv_recv.at[side, h], 0, (-1, 1)[side],
        )

    barrier = pltpu.get_barrier_semaphore()
    expected = jnp.int32(0)
    for there, dt, ds in ((left, 0, -1), (right, 0, 1), (earlier, -1, 0), (later, 1, 0)):
        expected = expected + there.astype(jnp.int32)

        @pl.when(there)
        def _(dt=dt, ds=ds):
            pl.semaphore_signal(barrier, inc=1, device_id=(t + dt, s + ds), device_id_type=MESH)

    own = [
        pltpu.make_async_copy(k_in.at[0], kv.at[0, n:2 * n], own_sem.at[0]),
        pltpu.make_async_copy(v_in.at[0], kv.at[1, n:2 * n], own_sem.at[1]),
        pltpu.make_async_copy(q_in.at[0], qg.at[0, :n], own_sem.at[2]),
        pltpu.make_async_copy(g_in.at[0], qg.at[1, :n], own_sem.at[3]),
    ]
    small = [
        pltpu.make_async_copy(mask_in, mask_ref, own_sem.at[4]),
        pltpu.make_async_copy(valid_in, valid_ref, own_sem.at[5]),
    ]
    for c in small + own:
        c.start()
    for c in small:
        c.wait()

    for c in range(3):
        gate[0, c:c + 1, :] = jnp.full((1, n), jnp.where(mask_ref[0, 0, 3 + c] == 1, 1.0, 0.0), jnp.float32)

    for c in own:
        c.wait()
    pl.semaphore_wait(barrier, expected)

    @pl.when(earlier)
    def _():
        gate_copy().start()

    @pl.loop(0, HEADS)
    def _(h):
        @pl.when(jnp.logical_and(earlier, h < AHEAD))
        def _():
            qg_copy(h).start()

        for side, (there, _) in enumerate(sides):
            @pl.when(there)
            def _(side=side):
                kv_copy(h, side).start()

    row = lax.broadcasted_iota(jnp.int32, (n, n), 0)
    frame_valid = valid_ref[t]

    def key_limit(c):
        near = s + c - 1
        inside = jnp.logical_and(near >= 0, near < blocks).astype(jnp.int32)
        return jnp.maximum(frame_valid - near * n, 0) * inside

    for c in range(3):
        limit = key_limit(c) * jnp.where(mask_ref[0, 0, c] == 1, 1, 0)
        bias[c * n:(c + 1) * n, :n] = jnp.where(row < limit, 0.0, -BIG)

    lane = lax.broadcasted_iota(jnp.int32, (1, 2 * n), 1)
    next_valid = valid_ref[jnp.minimum(t + 1, frames - 1)] * later.astype(jnp.int32)
    okay = jnp.where(lane < jnp.where(lane < n, jnp.minimum(frame_valid - s * n, n), next_valid - s * n + n), 1.0, 0.0)

    zeros = jnp.zeros((n, kv.shape[2]), kv.dtype)
    none = jnp.where(lax.broadcasted_iota(jnp.int32, (4, n), 0) == 0, -BIG, 0.0)
    for slot, there in ((0, left), (2, right)):
        @pl.when(jnp.logical_not(there))
        def _(slot=slot):
            for k in range(2):
                kv[k, slot * n:(slot + 1) * n, :] = zeros
            dkv_far[1 - slot // 2] = jnp.zeros(dkv_far.shape[1:], dkv_far.dtype)

    @pl.when(jnp.logical_not(later))
    def _():
        for k in range(2):
            qg[k, n:, :] = zeros
        gate[1] = jnp.zeros((4, n), jnp.float32)
        for h in range(HEADS):
            stat_far[h, :, n:] = none
            stat[h, :, n:] = jnp.ones((4, n), jnp.float32)
            e_all[h, :, n:] = jnp.zeros((3 * n, n), jnp.float32)
            d_all[h, :, n:] = jnp.zeros((3 * n, n), jnp.float32)

    @pl.when(jnp.logical_not(earlier))
    def _():
        dq_far[...] = jnp.zeros(dq_far.shape, dq_far.dtype)
        for h in range(HEADS):
            stat_far[h, :, :n] = none

    @pl.when(later)
    def _():
        gate_copy().wait_recv()

    for c in range(3):
        open_here = jnp.logical_and(row < key_limit(c), gate[1, c:c + 1, :] > 0.5)
        bias[c * n:(c + 1) * n, n:] = jnp.where(open_here, 0.0, -BIG)

    def scores(h, half):
        hc = cols(h)
        q = slice(half * n, (half + 1) * n)
        score = dot(kv[0, :, hc], qg[0, q, hc], NT) * scale2 + bias[:, q]
        peak = jnp.max(score, axis=0, keepdims=True)
        e = jnp.exp2(score - peak)
        dprob = dot(kv[1, :, hc], qg[1, q, hc], NT)
        e_all[h, :, q] = e
        d_all[h, :, q] = dprob
        stat[h, 0:1, q] = peak
        stat[h, 1:2, q] = jnp.sum(e, axis=0, keepdims=True)
        stat[h, 2:3, q] = jnp.sum(e * dprob, axis=0, keepdims=True)

    def own_scores(h):
        for side, (there, _) in enumerate(sides):
            @pl.when(there)
            def _(side=side):
                kv_copy(h, 1 - side).wait_recv()

        scores(h, 0)

        @pl.when(earlier)
        def _():
            stat_copy(h, 0).start()

    def next_scores(h):
        @pl.when(later)
        def _():
            qg_copy(h).wait_recv()
            scores(h, 1)
            stat_copy(h, 1).start()

    def grads(h):
        @pl.when(earlier)
        def _():
            stat_copy(h, 1).wait_recv()

        @pl.when(later)
        def _():
            stat_copy(h, 0).wait_recv()

        hc = cols(h)
        near, far = stat[h], stat_far[h]
        peak = jnp.maximum(near[0:1], far[0:1])
        a, b = jnp.exp2(near[0:1] - peak), jnp.exp2(far[0:1] - peak)
        norm = 1.0 / (near[1:2] * a + far[1:2] * b)
        row_dot = (near[2:3] * a + far[2:3] * b) * norm
        prob = e_all[h] * (okay * a * norm)
        query, grad, key = qg[0, :, hc], qg[1, :, hc], kv[0, :, hc]

        def send(k, part_of_h):
            home = (dk_home, dv_home)[k]
            home[:, hc] = part_of_h[n:2 * n]
            for side, (there, _) in enumerate(sides):
                part = part_of_h[2 * side * n:(2 * side + 1) * n]
                dkv_out[side, h, k * n:(k + 1) * n] = part.astype(dkv_out.dtype)

                @pl.when(there)
                def _(side=side):
                    dkv_half(h, side, k).start()

        send(1, dot(prob.astype(jnp.bfloat16), grad, NN))
        dscore = (prob * (d_all[h] - row_dot)).astype(jnp.bfloat16)
        send(0, dot(dscore, query, NN) * scale)
        dq = dot(dscore, key, TN) * scale
        dq_home[:, hc] = dq[:n]
        dq_out[h] = dq[n:].astype(dq_out.dtype)

        @pl.when(jnp.logical_and(later, jnp.logical_or(h < HELD, h > HELD_LAST)))
        def _():
            dq_copy(h).start()

    def sums(h):
        hc = cols(h)

        @pl.when(earlier)
        def _():
            dq_copy(h).wait_recv()

        dq_ref[0, :, hc] = (dq_home[:, hc] + dq_far[h].astype(jnp.float32)).astype(dq_ref.dtype)
        for side, (there, _) in enumerate(sides):
            @pl.when(there)
            def _(side=side):
                dkv_copy(h, 1 - side).wait_recv()
        from_right, from_left = dkv_far[0, h].astype(jnp.float32), dkv_far[1, h].astype(jnp.float32)
        both = from_right + from_left
        dk_ref[0, :, hc] = (dk_home[:, hc] + both[:n]).astype(dk_ref.dtype)
        dv_ref[0, :, hc] = (dv_home[:, hc] + both[n:]).astype(dv_ref.dtype)

    def inputs_sent(h):
        @pl.when(earlier)
        def _():
            qg_copy(h).wait_send()

        for side, (there, _) in enumerate(sides):
            @pl.when(there)
            def _(side=side):
                kv_copy(h, side).wait_send()

    def totals_sent(h):
        @pl.when(earlier)
        def _():
            stat_copy(h, 0).wait_send()

        @pl.when(later)
        def _():
            stat_copy(h, 1).wait_send()

    def grads_sent(h):
        @pl.when(later)
        def _():
            dq_copy(h).wait_send()

        for side, (there, _) in enumerate(sides):
            @pl.when(there)
            def _(side=side):
                dkv_copy(h, side).wait_send()

    @pl.loop(0, LEAD_OWN)
    def _(h):
        own_scores(h)

    lag = jnp.where(earlier, LAG_GRADS, LAG_FIRST)

    @pl.loop(0, HEADS + LAG_SUMS)
    def _(i):
        @pl.when(i < HEADS)
        def _():
            next_scores(i)

        @pl.when(jnp.logical_and(later, i == HEADS - 1))
        def _():
            for h in range(HELD, HELD_LAST + 1):
                dq_copy(h).start()

        @pl.when(jnp.logical_and(earlier, i < HEADS - AHEAD))
        def _():
            qg_copy(i + AHEAD).start()

        @pl.when(jnp.logical_and(i >= lag, i < HEADS + lag))
        def _():
            grads(i - lag)

        @pl.when(i < HEADS - LEAD_OWN)
        def _():
            own_scores(i + LEAD_OWN)

        @pl.when(i == HEADS + 1)
        def _():
            @pl.when(earlier)
            def _():
                gate_copy().wait_send()

            @pl.loop(0, HEADS)
            def _(h):
                inputs_sent(h)

        @pl.when(i == HEADS + 2)
        def _():
            @pl.loop(0, HEADS)
            def _(h):
                totals_sent(h)

        @pl.when(i >= LAG_SUMS)
        def _():
            sums(i - LAG_SUMS)
            grads_sent(i - LAG_SUMS)


def store(dq, dk, dv, dq_out, dk_out, dv_out, sem):
    copies = [
        pltpu.make_async_copy(src, dst, sem.at[k])
        for k, (src, dst) in enumerate(((dq, dq_out), (dk, dk_out), (dv, dv_out)))
    ]
    for c in copies:
        c.start()
    for c in copies:
        c.wait()


def solution(mesh):
    frames, blocks = mesh.shape["tm"], mesh.shape["seq"]

    def body(queries, keys, values, grad_out, block_mask, valid_len):
        _, n, feat = queries.shape
        hd = feat // HEADS
        out = jax.ShapeDtypeStruct(queries.shape, queries.dtype)
        vmem = pl.BlockSpec(memory_space=pltpu.VMEM)
        hbm = pl.BlockSpec(memory_space=pl.ANY)
        dma = pltpu.SemaphoreType.DMA
        held = pltpu.VMEM(queries.shape, queries.dtype)
        grads = pl.pallas_call(
            functools.partial(kernel, frames, blocks, n, hd),
            out_shape=(held,) * 3,
            in_specs=[hbm] * 6,
            out_specs=(vmem,) * 3,
            scratch_shapes=[
                pltpu.VMEM((2, 3 * n, feat), jnp.bfloat16),
                pltpu.VMEM((2, 2 * n, feat), jnp.bfloat16),
                pltpu.VMEM((3 * n, 2 * n), jnp.float32),
                pltpu.VMEM((2, 4, n), jnp.float32),
                pltpu.VMEM((HEADS, 3 * n, 2 * n), jnp.float32),
                pltpu.VMEM((HEADS, 3 * n, 2 * n), jnp.float32),
                pltpu.VMEM((HEADS, 4, 2 * n), jnp.float32),
                pltpu.VMEM((HEADS, 4, 2 * n), jnp.float32),
                pltpu.VMEM((n, feat), jnp.float32),
                pltpu.VMEM((n, feat), jnp.float32),
                pltpu.VMEM((n, feat), jnp.float32),
                pltpu.VMEM((HEADS, n, hd), jnp.bfloat16),
                pltpu.VMEM((HEADS, n, hd), jnp.bfloat16),
                pltpu.VMEM((2, HEADS, 2 * n, hd), jnp.bfloat16),
                pltpu.VMEM((2, HEADS, 2 * n, hd), jnp.bfloat16),
                pltpu.SMEM(block_mask.shape, jnp.int32),
                pltpu.SMEM(valid_len.shape, jnp.int32),
                dma((6,)),
                dma((2, HEADS)),
                dma((2, HEADS)),
                dma((HEADS,)),
                dma((HEADS,)),
                dma((2,)),
                dma((2, HEADS)),
                dma((2, HEADS)),
                dma((HEADS,)),
                dma((HEADS,)),
                dma((2, HEADS)),
                dma((2, HEADS)),
            ],
            compiler_params=pltpu.CompilerParams(collective_id=0, has_side_effects=True),
        )(keys, values, queries, grad_out, block_mask, valid_len)
        return pl.pallas_call(
            store,
            out_shape=(out,) * 3,
            in_specs=[vmem] * 3,
            out_specs=(hbm,) * 3,
            scratch_shapes=[dma((3,))],
        )(*(pltpu.with_memory_space_constraint(x, pltpu.VMEM) for x in grads))

    spec = P("tm", "seq", None)
    return jax.shard_map(
        body, mesh=mesh, in_specs=(spec,) * 5 + (P(),), out_specs=(spec,) * 3, check_vma=False
    )
```

```python
import functools
import math

import jax
import jax.numpy as jnp
from jax import lax
from jax.experimental import pallas as pl
from jax.experimental.pallas import tpu as pltpu
from jax.sharding import PartitionSpec as P

HEADS = 8
AHEAD = 4
HELD = 2
RELAY_LAG = 7
HELD_LAST = 3
LEAD_OWN = 3
LAG_GRADS = 3
LAG_FIRST = 2
LAG_SUMS = 10
BIG = 1e30
MESH = pl.DeviceIdType.MESH
NT = (((1,), (1,)), ((), ()))
TN = (((0,), (0,)), ((), ()))
NN = (((1,), (0,)), ((), ()))


def dot(a, b, dims):
    return lax.dot_general(a, b, dims, preferred_element_type=jnp.float32)


def kernel(
    frames, blocks, block_len, head_dim,
    k_in, v_in, q_in, g_in, mask_in, valid_in,
    dq_ref, dk_ref, dv_ref,
    kv, qg, bias, gate, e_all, d_all, peaks, stat, stat_far, dq_home, dk_home, dv_home,
    dq_out, dq_far, dkv_out, dkv_far, relay,
    mask_ref, valid_ref, own_sem, kv_send, kv_recv, qg_send, qg_recv, gate_sem, stat_send, stat_recv, dq_send, dq_recv, dkv_send, dkv_recv, relay_recv, relay_send,
):
    n = block_len
    t = lax.axis_index("tm")
    s = lax.axis_index("seq")
    scale = head_dim ** (-0.5)
    scale2 = scale * math.log2(math.e)
    left, right = s > 0, s < blocks - 1
    earlier, later = t > 0, t < frames - 1
    sides = ((left, -1), (right, 1))

    def cols(h):
        return pl.ds(pl.multiple_of(h * head_dim, head_dim), head_dim)

    def remote(src, dst, send, recv, dt, ds):
        return pltpu.make_async_remote_copy(
            src_ref=src, dst_ref=dst, send_sem=send, recv_sem=recv,
            device_id=(t + dt, s + ds), device_id_type=MESH,
        )

    def kv_copy(h, side):
        slot = 2 - 2 * side
        return remote(
            kv.at[:, n:2 * n, cols(h)], kv.at[:, slot * n:(slot + 1) * n, cols(h)],
            kv_send.at[side, h], kv_recv.at[side, h], 0, (-1, 1)[side],
        )

    def qg_copy(h):
        return remote(qg.at[:, :n, cols(h)], qg.at[:, n:, cols(h)], qg_send.at[h], qg_recv.at[h], -1, 0)

    def gate_copy():
        return remote(gate.at[0], gate.at[1], gate_sem.at[0], gate_sem.at[1], -1, 0)

    def stat_copy(h, up):
        src, dst = ((slice(0, n), slice(n, 2 * n)), (slice(n, 2 * n), slice(0, n)))[up]
        return remote(
            stat.at[h, :, src], stat_far.at[h, :, dst], stat_send.at[up, h], stat_recv.at[up, h], (-1, 1)[up], 0
        )

    def dq_copy(h):
        return remote(dq_out.at[h], dq_far.at[h], dq_send.at[h], dq_recv.at[h], 1, 0)

    square = frames == 4
    round_about = t == 1 if square else t < 0

    def dq_first(h):
        return remote(dq_out.at[h], relay.at[h - HELD], dq_send.at[h], relay_recv.at[h - HELD], 2, 0)

    def dq_second(h):
        return remote(relay.at[h - HELD], dq_far.at[h], relay_send.at[h - HELD], dq_recv.at[h], -1, 0)

    def dkv_copy(h, side):
        return remote(
            dkv_out.at[side, h], dkv_far.at[side, h], dkv_send.at[side, h], dkv_recv.at[side, h], 0, (-1, 1)[side]
        )

    def dkv_half(h, side, k):
        rows = slice(k * n, (k + 1) * n)
        return remote(
            dkv_out.at[side, h, rows], dkv_far.at[side, h, rows],
            dkv_send.at[side, h], dkv_recv.at[side, h], 0, (-1, 1)[side],
        )

    barrier = pltpu.get_barrier_semaphore()
    expected = jnp.int32(0)
    for there, dt, ds in ((left, 0, -1), (right, 0, 1), (earlier, -1, 0), (later, 1, 0)):
        expected = expected + there.astype(jnp.int32)

        @pl.when(there)
        def _(dt=dt, ds=ds):
            pl.semaphore_signal(barrier, inc=1, device_id=(t + dt, s + ds), device_id_type=MESH)

    if square:
        expected = expected + round_about.astype(jnp.int32)

        @pl.when(t == 3)
        def _():
            pl.semaphore_signal(barrier, inc=1, device_id=(t - 2, s), device_id_type=MESH)

    own = [
        pltpu.make_async_copy(k_in.at[0], kv.at[0, n:2 * n], own_sem.at[0]),
        pltpu.make_async_copy(v_in.at[0], kv.at[1, n:2 * n], own_sem.at[1]),
        pltpu.make_async_copy(q_in.at[0], qg.at[0, :n], own_sem.at[2]),
        pltpu.make_async_copy(g_in.at[0], qg.at[1, :n], own_sem.at[3]),
    ]
    small = [
        pltpu.make_async_copy(mask_in, mask_ref, own_sem.at[4]),
        pltpu.make_async_copy(valid_in, valid_ref, own_sem.at[5]),
    ]
    for c in small + own:
        c.start()
    for c in small:
        c.wait()

    for c in range(3):
        gate[0, c:c + 1, :] = jnp.full((1, n), jnp.where(mask_ref[0, 0, 3 + c] == 1, 1.0, 0.0), jnp.float32)

    for c in own:
        c.wait()
    pl.semaphore_wait(barrier, expected)

    @pl.when(earlier)
    def _():
        gate_copy().start()

    @pl.loop(0, HEADS)
    def _(h):
        @pl.when(jnp.logical_and(earlier, h < AHEAD))
        def _():
            qg_copy(h).start()

        for side, (there, _) in enumerate(sides):
            @pl.when(there)
            def _(side=side):
                kv_copy(h, side).start()

    row = lax.broadcasted_iota(jnp.int32, (n, n), 0)
    frame_valid = valid_ref[t]

    def key_limit(c):
        near = s + c - 1
        inside = jnp.logical_and(near >= 0, near < blocks).astype(jnp.int32)
        return jnp.maximum(frame_valid - near * n, 0) * inside

    for c in range(3):
        limit = key_limit(c) * jnp.where(mask_ref[0, 0, c] == 1, 1, 0)
        bias[c * n:(c + 1) * n, :n] = jnp.where(row < limit, 0.0, -BIG)

    lane = lax.broadcasted_iota(jnp.int32, (1, 2 * n), 1)
    next_valid = valid_ref[jnp.minimum(t + 1, frames - 1)] * later.astype(jnp.int32)
    okay = jnp.where(lane < jnp.where(lane < n, jnp.minimum(frame_valid - s * n, n), next_valid - s * n + n), 1.0, 0.0)

    zeros = jnp.zeros((n, kv.shape[2]), kv.dtype)
    none = jnp.where(lax.broadcasted_iota(jnp.int32, (2, n), 0) == 0, -BIG, 0.0)
    for slot, there in ((0, left), (2, right)):
        @pl.when(jnp.logical_not(there))
        def _(slot=slot):
            for k in range(2):
                kv[k, slot * n:(slot + 1) * n, :] = zeros
            dkv_far[1 - slot // 2] = jnp.zeros(dkv_far.shape[1:], dkv_far.dtype)

    @pl.when(jnp.logical_not(later))
    def _():
        for k in range(2):
            qg[k, n:, :] = zeros
        gate[1] = jnp.zeros((4, n), jnp.float32)
        for h in range(HEADS):
            stat_far[h, :, n:] = none
            stat[h, :, n:] = jnp.zeros((2, n), jnp.float32)
            peaks[h, :, n:] = jnp.zeros((1, n), jnp.float32)
            e_all[h, :, n:] = jnp.zeros((3 * n, n), jnp.float32)
            d_all[h, :, n:] = jnp.zeros((3 * n, n), jnp.float32)

    @pl.when(jnp.logical_not(earlier))
    def _():
        dq_far[...] = jnp.zeros(dq_far.shape, dq_far.dtype)
        for h in range(HEADS):
            stat_far[h, :, :n] = none

    @pl.when(later)
    def _():
        gate_copy().wait_recv()

    for c in range(3):
        open_here = jnp.logical_and(row < key_limit(c), gate[1, c:c + 1, :] > 0.5)
        bias[c * n:(c + 1) * n, n:] = jnp.where(open_here, 0.0, -BIG)

    def scores(h, half):
        hc = cols(h)
        q = slice(half * n, (half + 1) * n)
        score = dot(kv[0, :, hc], qg[0, q, hc], NT) * scale2 + bias[:, q]
        peak = jnp.max(score, axis=0, keepdims=True)
        e = jnp.exp2(score - peak)
        dprob = dot(kv[1, :, hc], qg[1, q, hc], NT)
        e_all[h, :, q] = e
        d_all[h, :, q] = dprob
        total = jnp.sum(e, axis=0, keepdims=True)
        peaks[h, :, q] = peak
        stat[h, 0:1, q] = peak + jnp.log2(total)
        stat[h, 1:2, q] = jnp.sum(e * dprob, axis=0, keepdims=True) / total

    def own_scores(h):
        for side, (there, _) in enumerate(sides):
            @pl.when(there)
            def _(side=side):
                kv_copy(h, 1 - side).wait_recv()

        scores(h, 0)

        @pl.when(earlier)
        def _():
            stat_copy(h, 0).start()

    def next_scores(h):
        @pl.when(later)
        def _():
            qg_copy(h).wait_recv()
            scores(h, 1)
            stat_copy(h, 1).start()

    def grads(h):
        @pl.when(earlier)
        def _():
            stat_copy(h, 1).wait_recv()

        @pl.when(later)
        def _():
            stat_copy(h, 0).wait_recv()

        hc = cols(h)
        near, far = stat[h], stat_far[h]
        top = jnp.maximum(near[0:1], far[0:1])
        a, b = jnp.exp2(near[0:1] - top), jnp.exp2(far[0:1] - top)
        row_dot = (near[1:2] * a + far[1:2] * b) / (a + b)
        prob = e_all[h] * (okay * jnp.exp2(peaks[h] - (top + jnp.log2(a + b))))
        query, grad, key = qg[0, :, hc], qg[1, :, hc], kv[0, :, hc]

        def send(k, part_of_h):
            home = (dk_home, dv_home)[k]
            home[:, hc] = part_of_h[n:2 * n]
            for side, (there, _) in enumerate(sides):
                part = part_of_h[2 * side * n:(2 * side + 1) * n]
                dkv_out[side, h, k * n:(k + 1) * n] = part.astype(dkv_out.dtype)

                @pl.when(there)
                def _(side=side):
                    dkv_half(h, side, k).start()

        send(1, dot(prob.astype(jnp.bfloat16), grad, NN))
        dscore = (prob * (d_all[h] - row_dot)).astype(jnp.bfloat16)
        send(0, dot(dscore, query, NN) * scale)
        dq = dot(dscore, key, TN) * scale
        dq_home[:, hc] = dq[:n]
        dq_out[h] = dq[n:].astype(dq_out.dtype)

        @pl.when(jnp.logical_and(later, jnp.logical_or(h < HELD, h > HELD_LAST)))
        def _():
            dq_copy(h).start()

        if square:
            @pl.when(jnp.logical_and(round_about, jnp.logical_and(h >= HELD, h <= HELD_LAST)))
            def _():
                dq_first(h).start()

    def sums(h):
        hc = cols(h)

        @pl.when(earlier)
        def _():
            dq_copy(h).wait_recv()

        dq_ref[0, :, hc] = (dq_home[:, hc] + dq_far[h].astype(jnp.float32)).astype(dq_ref.dtype)
        for side, (there, _) in enumerate(sides):
            @pl.when(there)
            def _(side=side):
                dkv_copy(h, 1 - side).wait_recv()
        from_right, from_left = dkv_far[0, h].astype(jnp.float32), dkv_far[1, h].astype(jnp.float32)
        both = from_right + from_left
        dk_ref[0, :, hc] = (dk_home[:, hc] + both[:n]).astype(dk_ref.dtype)
        dv_ref[0, :, hc] = (dv_home[:, hc] + both[n:]).astype(dv_ref.dtype)

    def inputs_sent(h):
        @pl.when(earlier)
        def _():
            qg_copy(h).wait_send()

        for side, (there, _) in enumerate(sides):
            @pl.when(there)
            def _(side=side):
                kv_copy(h, side).wait_send()

    def totals_sent(h):
        @pl.when(earlier)
        def _():
            stat_copy(h, 0).wait_send()

        @pl.when(later)
        def _():
            stat_copy(h, 1).wait_send()

    def grads_sent(h):
        @pl.when(later)
        def _():
            dq_copy(h).wait_send()

        for side, (there, _) in enumerate(sides):
            @pl.when(there)
            def _(side=side):
                dkv_copy(h, side).wait_send()

    @pl.loop(0, LEAD_OWN)
    def _(h):
        own_scores(h)

    lag = jnp.where(earlier, LAG_GRADS, LAG_FIRST)

    @pl.loop(0, HEADS + LAG_SUMS)
    def _(i):
        @pl.when(i < HEADS)
        def _():
            next_scores(i)

        @pl.when(jnp.logical_and(jnp.logical_and(later, jnp.logical_not(round_about)), i == HEADS - 1))
        def _():
            for h in range(HELD, HELD_LAST + 1):
                dq_copy(h).start()

        @pl.when(jnp.logical_and(earlier, i < HEADS - AHEAD))
        def _():
            qg_copy(i + AHEAD).start()

        @pl.when(jnp.logical_and(i >= lag, i < HEADS + lag))
        def _():
            grads(i - lag)

        if square:
            @pl.when(jnp.logical_and(t == 3, jnp.logical_and(i >= HELD + RELAY_LAG, i <= HELD_LAST + RELAY_LAG)))
            def _():
                dq_first(i - RELAY_LAG).wait_recv()
                dq_second(i - RELAY_LAG).start()

        @pl.when(i < HEADS - LEAD_OWN)
        def _():
            own_scores(i + LEAD_OWN)

        @pl.when(i == HEADS + 1)
        def _():
            @pl.when(earlier)
            def _():
                gate_copy().wait_send()

            @pl.loop(0, HEADS)
            def _(h):
                inputs_sent(h)

        if square:
            @pl.when(jnp.logical_and(t == 3, i == HEADS + LAG_SUMS - 1))
            def _():
                for h in range(HELD, HELD_LAST + 1):
                    dq_second(h).wait_send()

        @pl.when(i == HEADS + 2)
        def _():
            @pl.loop(0, HEADS)
            def _(h):
                totals_sent(h)

        @pl.when(i >= LAG_SUMS)
        def _():
            sums(i - LAG_SUMS)
            grads_sent(i - LAG_SUMS)


def store(dq, dk, dv, dq_out, dk_out, dv_out, sem):
    copies = [
        pltpu.make_async_copy(src, dst, sem.at[k])
        for k, (src, dst) in enumerate(((dq, dq_out), (dk, dk_out), (dv, dv_out)))
    ]
    for c in copies:
        c.start()
    for c in copies:
        c.wait()


def solution(mesh):
    frames, blocks = mesh.shape["tm"], mesh.shape["seq"]

    def body(queries, keys, values, grad_out, block_mask, valid_len):
        _, n, feat = queries.shape
        hd = feat // HEADS
        out = jax.ShapeDtypeStruct(queries.shape, queries.dtype)
        vmem = pl.BlockSpec(memory_space=pltpu.VMEM)
        hbm = pl.BlockSpec(memory_space=pl.ANY)
        dma = pltpu.SemaphoreType.DMA
        held = pltpu.VMEM(queries.shape, queries.dtype)
        grads = pl.pallas_call(
            functools.partial(kernel, frames, blocks, n, hd),
            out_shape=(held,) * 3,
            in_specs=[hbm] * 6,
            out_specs=(vmem,) * 3,
            scratch_shapes=[
                pltpu.VMEM((2, 3 * n, feat), jnp.bfloat16),
                pltpu.VMEM((2, 2 * n, feat), jnp.bfloat16),
                pltpu.VMEM((3 * n, 2 * n), jnp.float32),
                pltpu.VMEM((2, 4, n), jnp.float32),
                pltpu.VMEM((HEADS, 3 * n, 2 * n), jnp.float32),
                pltpu.VMEM((HEADS, 3 * n, 2 * n), jnp.float32),
                pltpu.VMEM((HEADS, 1, 2 * n), jnp.float32),
                pltpu.VMEM((HEADS, 2, 2 * n), jnp.float32),
                pltpu.VMEM((HEADS, 2, 2 * n), jnp.float32),
                pltpu.VMEM((n, feat), jnp.float32),
                pltpu.VMEM((n, feat), jnp.float32),
                pltpu.VMEM((n, feat), jnp.float32),
                pltpu.VMEM((HEADS, n, hd), jnp.bfloat16),
                pltpu.VMEM((HEADS, n, hd), jnp.bfloat16),
                pltpu.VMEM((2, HEADS, 2 * n, hd), jnp.bfloat16),
                pltpu.VMEM((2, HEADS, 2 * n, hd), jnp.bfloat16),
                pltpu.VMEM((HELD_LAST + 1 - HELD, n, hd), jnp.bfloat16),
                pltpu.SMEM(block_mask.shape, jnp.int32),
                pltpu.SMEM(valid_len.shape, jnp.int32),
                dma((6,)),
                dma((2, HEADS)),
                dma((2, HEADS)),
                dma((HEADS,)),
                dma((HEADS,)),
                dma((2,)),
                dma((2, HEADS)),
                dma((2, HEADS)),
                dma((HEADS,)),
                dma((HEADS,)),
                dma((2, HEADS)),
                dma((2, HEADS)),
                dma((HELD_LAST + 1 - HELD,)),
                dma((HELD_LAST + 1 - HELD,)),
            ],
            compiler_params=pltpu.CompilerParams(collective_id=0, has_side_effects=True),
        )(keys, values, queries, grad_out, block_mask, valid_len)
        return pl.pallas_call(
            store,
            out_shape=(out,) * 3,
            in_specs=[vmem] * 3,
            out_specs=(hbm,) * 3,
            scratch_shapes=[dma((3,))],
        )(*(pltpu.with_memory_space_constraint(x, pltpu.VMEM) for x in grads))

    spec = P("tm", "seq", None)
    return jax.shard_map(
        body, mesh=mesh, in_specs=(spec,) * 5 + (P(),), out_specs=(spec,) * 3, check_vma=False
    )
```

```python
import functools
import math

import jax
import jax.numpy as jnp
from jax import lax
from jax.experimental import pallas as pl
from jax.experimental.pallas import tpu as pltpu
from jax.sharding import PartitionSpec as P

HEADS = 8
AHEAD = 4
HELD = 2
RELAY_LAG = 7
VIA = 5
HELD_LAST = 3
LEAD_OWN = 3
LAG_GRADS = 3
LAG_FIRST = 2
LAG_SUMS = 10
BIG = 1e30
MESH = pl.DeviceIdType.MESH
NT = (((1,), (1,)), ((), ()))
TN = (((0,), (0,)), ((), ()))
NN = (((1,), (0,)), ((), ()))


def dot(a, b, dims):
    return lax.dot_general(a, b, dims, preferred_element_type=jnp.float32)


def kernel(
    frames, blocks, block_len, head_dim,
    k_in, v_in, q_in, g_in, mask_in, valid_in,
    dq_ref, dk_ref, dv_ref,
    kv, qg, bias, gate, e_all, d_all, peaks, stat, stat_far, dq_home, dk_home, dv_home,
    dq_out, dq_far, dkv_out, dkv_far, relay, qg_relay,
    mask_ref, valid_ref, own_sem, kv_send, kv_recv, qg_send, qg_recv, gate_sem, stat_send, stat_recv, dq_send, dq_recv, dkv_send, dkv_recv, relay_recv, relay_send, via_recv, via_send,
):
    n = block_len
    t = lax.axis_index("tm")
    s = lax.axis_index("seq")
    scale = head_dim ** (-0.5)
    scale2 = scale * math.log2(math.e)
    left, right = s > 0, s < blocks - 1
    earlier, later = t > 0, t < frames - 1
    sides = ((left, -1), (right, 1))

    def cols(h):
        return pl.ds(pl.multiple_of(h * head_dim, head_dim), head_dim)

    def remote(src, dst, send, recv, dt, ds):
        return pltpu.make_async_remote_copy(
            src_ref=src, dst_ref=dst, send_sem=send, recv_sem=recv,
            device_id=(t + dt, s + ds), device_id_type=MESH,
        )

    def kv_copy(h, side):
        slot = 2 - 2 * side
        return remote(
            kv.at[:, n:2 * n, cols(h)], kv.at[:, slot * n:(slot + 1) * n, cols(h)],
            kv_send.at[side, h], kv_recv.at[side, h], 0, (-1, 1)[side],
        )

    def qg_copy(h):
        return remote(qg.at[:, :n, cols(h)], qg.at[:, n:, cols(h)], qg_send.at[h], qg_recv.at[h], -1, 0)

    def gate_copy():
        return remote(gate.at[0], gate.at[1], gate_sem.at[0], gate_sem.at[1], -1, 0)

    def stat_copy(h, up):
        src, dst = ((slice(0, n), slice(n, 2 * n)), (slice(n, 2 * n), slice(0, n)))[up]
        return remote(
            stat.at[h, :, src], stat_far.at[h, :, dst], stat_send.at[up, h], stat_recv.at[up, h], (-1, 1)[up], 0
        )

    def dq_copy(h):
        return remote(dq_out.at[h], dq_far.at[h], dq_send.at[h], dq_recv.at[h], 1, 0)

    square = frames == 4
    round_about = t == 1 if square else t < 0

    def qg_first(h):
        return remote(qg.at[:, :n, cols(h)], qg_relay.at[h - VIA], qg_send.at[h], via_recv.at[h - VIA], -2, 0)

    def qg_second(h):
        return remote(qg_relay.at[h - VIA], qg.at[:, n:, cols(h)], via_send.at[h - VIA], qg_recv.at[h], 1, 0)

    def dq_first(h):
        return remote(dq_out.at[h], relay.at[h - HELD], dq_send.at[h], relay_recv.at[h - HELD], 2, 0)

    def dq_second(h):
        return remote(relay.at[h - HELD], dq_far.at[h], relay_send.at[h - HELD], dq_recv.at[h], -1, 0)

    def dkv_copy(h, side):
        return remote(
            dkv_out.at[side, h], dkv_far.at[side, h], dkv_send.at[side, h], dkv_recv.at[side, h], 0, (-1, 1)[side]
        )

    def dkv_half(h, side, k):
        rows = slice(k * n, (k + 1) * n)
        return remote(
            dkv_out.at[side, h, rows], dkv_far.at[side, h, rows],
            dkv_send.at[side, h], dkv_recv.at[side, h], 0, (-1, 1)[side],
        )

    barrier = pltpu.get_barrier_semaphore()
    expected = jnp.int32(0)
    for there, dt, ds in ((left, 0, -1), (right, 0, 1), (earlier, -1, 0), (later, 1, 0)):
        expected = expected + there.astype(jnp.int32)

        @pl.when(there)
        def _(dt=dt, ds=ds):
            pl.semaphore_signal(barrier, inc=1, device_id=(t + dt, s + ds), device_id_type=MESH)

    if square:
        expected = expected + jnp.logical_or(round_about, t == 2).astype(jnp.int32)

        @pl.when(t == 0)
        def _():
            pl.semaphore_signal(barrier, inc=1, device_id=(t + 2, s), device_id_type=MESH)

        @pl.when(t == 3)
        def _():
            pl.semaphore_signal(barrier, inc=1, device_id=(t - 2, s), device_id_type=MESH)

    own = [
        pltpu.make_async_copy(k_in.at[0], kv.at[0, n:2 * n], own_sem.at[0]),
        pltpu.make_async_copy(v_in.at[0], kv.at[1, n:2 * n], own_sem.at[1]),
        pltpu.make_async_copy(q_in.at[0], qg.at[0, :n], own_sem.at[2]),
        pltpu.make_async_copy(g_in.at[0], qg.at[1, :n], own_sem.at[3]),
    ]
    small = [
        pltpu.make_async_copy(mask_in, mask_ref, own_sem.at[4]),
        pltpu.make_async_copy(valid_in, valid_ref, own_sem.at[5]),
    ]
    for c in small + own:
        c.start()
    for c in small:
        c.wait()

    for c in range(3):
        gate[0, c:c + 1, :] = jnp.full((1, n), jnp.where(mask_ref[0, 0, 3 + c] == 1, 1.0, 0.0), jnp.float32)

    for c in own:
        c.wait()
    pl.semaphore_wait(barrier, expected)

    @pl.when(earlier)
    def _():
        gate_copy().start()

    if square:
        @pl.when(t == 2)
        def _():
            for h in range(VIA, HEADS):
                qg_first(h).start()

    @pl.loop(0, HEADS)
    def _(h):
        @pl.when(jnp.logical_and(earlier, h < AHEAD))
        def _():
            qg_copy(h).start()

        for side, (there, _) in enumerate(sides):
            @pl.when(there)
            def _(side=side):
                kv_copy(h, side).start()

    row = lax.broadcasted_iota(jnp.int32, (n, n), 0)
    frame_valid = valid_ref[t]

    def key_limit(c):
        near = s + c - 1
        inside = jnp.logical_and(near >= 0, near < blocks).astype(jnp.int32)
        return jnp.maximum(frame_valid - near * n, 0) * inside

    for c in range(3):
        limit = key_limit(c) * jnp.where(mask_ref[0, 0, c] == 1, 1, 0)
        bias[c * n:(c + 1) * n, :n] = jnp.where(row < limit, 0.0, -BIG)

    lane = lax.broadcasted_iota(jnp.int32, (1, 2 * n), 1)
    next_valid = valid_ref[jnp.minimum(t + 1, frames - 1)] * later.astype(jnp.int32)
    okay = jnp.where(lane < jnp.where(lane < n, jnp.minimum(frame_valid - s * n, n), next_valid - s * n + n), 1.0, 0.0)

    zeros = jnp.zeros((n, kv.shape[2]), kv.dtype)
    none = jnp.where(lax.broadcasted_iota(jnp.int32, (2, n), 0) == 0, -BIG, 0.0)
    for slot, there in ((0, left), (2, right)):
        @pl.when(jnp.logical_not(there))
        def _(slot=slot):
            for k in range(2):
                kv[k, slot * n:(slot + 1) * n, :] = zeros
            dkv_far[1 - slot // 2] = jnp.zeros(dkv_far.shape[1:], dkv_far.dtype)

    @pl.when(jnp.logical_not(later))
    def _():
        for k in range(2):
            qg[k, n:, :] = zeros
        gate[1] = jnp.zeros((4, n), jnp.float32)
        for h in range(HEADS):
            stat_far[h, :, n:] = none
            stat[h, :, n:] = jnp.zeros((2, n), jnp.float32)
            peaks[h, :, n:] = jnp.zeros((1, n), jnp.float32)
            e_all[h, :, n:] = jnp.zeros((3 * n, n), jnp.float32)
            d_all[h, :, n:] = jnp.zeros((3 * n, n), jnp.float32)

    @pl.when(jnp.logical_not(earlier))
    def _():
        dq_far[...] = jnp.zeros(dq_far.shape, dq_far.dtype)
        for h in range(HEADS):
            stat_far[h, :, :n] = none

    @pl.when(later)
    def _():
        gate_copy().wait_recv()

    for c in range(3):
        open_here = jnp.logical_and(row < key_limit(c), gate[1, c:c + 1, :] > 0.5)
        bias[c * n:(c + 1) * n, n:] = jnp.where(open_here, 0.0, -BIG)

    def scores(h, half):
        hc = cols(h)
        q = slice(half * n, (half + 1) * n)
        score = dot(kv[0, :, hc], qg[0, q, hc], NT) * scale2 + bias[:, q]
        peak = jnp.max(score, axis=0, keepdims=True)
        e = jnp.exp2(score - peak)
        dprob = dot(kv[1, :, hc], qg[1, q, hc], NT)
        e_all[h, :, q] = e
        d_all[h, :, q] = dprob
        total = jnp.sum(e, axis=0, keepdims=True)
        peaks[h, :, q] = peak
        stat[h, 0:1, q] = peak + jnp.log2(total)
        stat[h, 1:2, q] = jnp.sum(e * dprob, axis=0, keepdims=True) / total

    def own_scores(h):
        for side, (there, _) in enumerate(sides):
            @pl.when(there)
            def _(side=side):
                kv_copy(h, 1 - side).wait_recv()

        scores(h, 0)

        @pl.when(earlier)
        def _():
            stat_copy(h, 0).start()

    def next_scores(h):
        @pl.when(later)
        def _():
            qg_copy(h).wait_recv()
            scores(h, 1)
            stat_copy(h, 1).start()

    def grads(h):
        @pl.when(earlier)
        def _():
            stat_copy(h, 1).wait_recv()

        @pl.when(later)
        def _():
            stat_copy(h, 0).wait_recv()

        hc = cols(h)
        near, far = stat[h], stat_far[h]
        top = jnp.maximum(near[0:1], far[0:1])
        a, b = jnp.exp2(near[0:1] - top), jnp.exp2(far[0:1] - top)
        row_dot = (near[1:2] * a + far[1:2] * b) / (a + b)
        prob = e_all[h] * (okay * jnp.exp2(peaks[h] - (top + jnp.log2(a + b))))
        query, grad, key = qg[0, :, hc], qg[1, :, hc], kv[0, :, hc]

        def send(k, part_of_h):
            home = (dk_home, dv_home)[k]
            home[:, hc] = part_of_h[n:2 * n]
            for side, (there, _) in enumerate(sides):
                part = part_of_h[2 * side * n:(2 * side + 1) * n]
                dkv_out[side, h, k * n:(k + 1) * n] = part.astype(dkv_out.dtype)

                @pl.when(there)
                def _(side=side):
                    dkv_half(h, side, k).start()

        send(1, dot(prob.astype(jnp.bfloat16), grad, NN))
        dscore = (prob * (d_all[h] - row_dot)).astype(jnp.bfloat16)
        send(0, dot(dscore, query, NN) * scale)
        dq = dot(dscore, key, TN) * scale
        dq_home[:, hc] = dq[:n]
        dq_out[h] = dq[n:].astype(dq_out.dtype)

        @pl.when(jnp.logical_and(later, jnp.logical_or(h < HELD, h > HELD_LAST)))
        def _():
            dq_copy(h).start()

        if square:
            @pl.when(jnp.logical_and(round_about, jnp.logical_and(h >= HELD, h <= HELD_LAST)))
            def _():
                dq_first(h).start()

    def sums(h):
        hc = cols(h)

        @pl.when(earlier)
        def _():
            dq_copy(h).wait_recv()

        dq_ref[0, :, hc] = (dq_home[:, hc] + dq_far[h].astype(jnp.float32)).astype(dq_ref.dtype)
        for side, (there, _) in enumerate(sides):
            @pl.when(there)
            def _(side=side):
                dkv_copy(h, 1 - side).wait_recv()
        from_right, from_left = dkv_far[0, h].astype(jnp.float32), dkv_far[1, h].astype(jnp.float32)
        both = from_right + from_left
        dk_ref[0, :, hc] = (dk_home[:, hc] + both[:n]).astype(dk_ref.dtype)
        dv_ref[0, :, hc] = (dv_home[:, hc] + both[n:]).astype(dv_ref.dtype)

    def inputs_sent(h):
        @pl.when(earlier)
        def _():
            qg_copy(h).wait_send()

        for side, (there, _) in enumerate(sides):
            @pl.when(there)
            def _(side=side):
                kv_copy(h, side).wait_send()

    def totals_sent(h):
        @pl.when(earlier)
        def _():
            stat_copy(h, 0).wait_send()

        @pl.when(later)
        def _():
            stat_copy(h, 1).wait_send()

    def grads_sent(h):
        @pl.when(later)
        def _():
            dq_copy(h).wait_send()

        for side, (there, _) in enumerate(sides):
            @pl.when(there)
            def _(side=side):
                dkv_copy(h, side).wait_send()

    @pl.loop(0, LEAD_OWN)
    def _(h):
        own_scores(h)

    lag = jnp.where(earlier, LAG_GRADS, LAG_FIRST)

    @pl.loop(0, HEADS + LAG_SUMS)
    def _(i):
        @pl.when(i < HEADS)
        def _():
            next_scores(i)

        @pl.when(jnp.logical_and(jnp.logical_and(later, jnp.logical_not(round_about)), i == HEADS - 1))
        def _():
            for h in range(HELD, HELD_LAST + 1):
                dq_copy(h).start()

        if square:
            @pl.when(jnp.logical_and(t == 0, i < HEADS - VIA))
            def _():
                qg_first(i + VIA).wait_recv()
                qg_second(i + VIA).start()

        ahead = jnp.where(t == 2, VIA, HEADS) if square else HEADS

        @pl.when(jnp.logical_and(earlier, i < ahead - AHEAD))
        def _():
            qg_copy(i + AHEAD).start()

        @pl.when(jnp.logical_and(i >= lag, i < HEADS + lag))
        def _():
            grads(i - lag)

        if square:
            @pl.when(jnp.logical_and(t == 3, jnp.logical_and(i >= HELD + RELAY_LAG, i <= HELD_LAST + RELAY_LAG)))
            def _():
                dq_first(i - RELAY_LAG).wait_recv()
                dq_second(i - RELAY_LAG).start()

        @pl.when(i < HEADS - LEAD_OWN)
        def _():
            own_scores(i + LEAD_OWN)

        @pl.when(i == HEADS + 1)
        def _():
            @pl.when(earlier)
            def _():
                gate_copy().wait_send()

            @pl.loop(0, HEADS)
            def _(h):
                inputs_sent(h)

        if square:
            @pl.when(jnp.logical_and(t == 3, i == HEADS + LAG_SUMS - 1))
            def _():
                for h in range(HELD, HELD_LAST + 1):
                    dq_second(h).wait_send()

            @pl.when(jnp.logical_and(t == 0, i == HEADS + 1))
            def _():
                for h in range(VIA, HEADS):
                    qg_second(h).wait_send()

        @pl.when(i == HEADS + 2)
        def _():
            @pl.loop(0, HEADS)
            def _(h):
                totals_sent(h)

        @pl.when(i >= LAG_SUMS)
        def _():
            sums(i - LAG_SUMS)
            grads_sent(i - LAG_SUMS)


def store(dq, dk, dv, dq_out, dk_out, dv_out, sem):
    copies = [
        pltpu.make_async_copy(src, dst, sem.at[k])
        for k, (src, dst) in enumerate(((dq, dq_out), (dk, dk_out), (dv, dv_out)))
    ]
    for c in copies:
        c.start()
    for c in copies:
        c.wait()


def solution(mesh):
    frames, blocks = mesh.shape["tm"], mesh.shape["seq"]

    def body(queries, keys, values, grad_out, block_mask, valid_len):
        _, n, feat = queries.shape
        hd = feat // HEADS
        out = jax.ShapeDtypeStruct(queries.shape, queries.dtype)
        vmem = pl.BlockSpec(memory_space=pltpu.VMEM)
        hbm = pl.BlockSpec(memory_space=pl.ANY)
        dma = pltpu.SemaphoreType.DMA
        held = pltpu.VMEM(queries.shape, queries.dtype)
        grads = pl.pallas_call(
            functools.partial(kernel, frames, blocks, n, hd),
            out_shape=(held,) * 3,
            in_specs=[hbm] * 6,
            out_specs=(vmem,) * 3,
            scratch_shapes=[
                pltpu.VMEM((2, 3 * n, feat), jnp.bfloat16),
                pltpu.VMEM((2, 2 * n, feat), jnp.bfloat16),
                pltpu.VMEM((3 * n, 2 * n), jnp.float32),
                pltpu.VMEM((2, 4, n), jnp.float32),
                pltpu.VMEM((HEADS, 3 * n, 2 * n), jnp.float32),
                pltpu.VMEM((HEADS, 3 * n, 2 * n), jnp.float32),
                pltpu.VMEM((HEADS, 1, 2 * n), jnp.float32),
                pltpu.VMEM((HEADS, 2, 2 * n), jnp.float32),
                pltpu.VMEM((HEADS, 2, 2 * n), jnp.float32),
                pltpu.VMEM((n, feat), jnp.float32),
                pltpu.VMEM((n, feat), jnp.float32),
                pltpu.VMEM((n, feat), jnp.float32),
                pltpu.VMEM((HEADS, n, hd), jnp.bfloat16),
                pltpu.VMEM((HEADS, n, hd), jnp.bfloat16),
                pltpu.VMEM((2, HEADS, 2 * n, hd), jnp.bfloat16),
                pltpu.VMEM((2, HEADS, 2 * n, hd), jnp.bfloat16),
                pltpu.VMEM((HELD_LAST + 1 - HELD, n, hd), jnp.bfloat16),
                pltpu.VMEM((HEADS - VIA, 2, n, hd), jnp.bfloat16),
                pltpu.SMEM(block_mask.shape, jnp.int32),
                pltpu.SMEM(valid_len.shape, jnp.int32),
                dma((6,)),
                dma((2, HEADS)),
                dma((2, HEADS)),
                dma((HEADS,)),
                dma((HEADS,)),
                dma((2,)),
                dma((2, HEADS)),
                dma((2, HEADS)),
                dma((HEADS,)),
                dma((HEADS,)),
                dma((2, HEADS)),
                dma((2, HEADS)),
                dma((HELD_LAST + 1 - HELD,)),
                dma((HELD_LAST + 1 - HELD,)),
                dma((HEADS - VIA,)),
                dma((HEADS - VIA,)),
            ],
            compiler_params=pltpu.CompilerParams(collective_id=0, has_side_effects=True),
        )(keys, values, queries, grad_out, block_mask, valid_len)
        return pl.pallas_call(
            store,
            out_shape=(out,) * 3,
            in_specs=[vmem] * 3,
            out_specs=(hbm,) * 3,
            scratch_shapes=[dma((3,))],
        )(*(pltpu.with_memory_space_constraint(x, pltpu.VMEM) for x in grads))

    spec = P("tm", "seq", None)
    return jax.shard_map(
        body, mesh=mesh, in_specs=(spec,) * 5 + (P(),), out_specs=(spec,) * 3, check_vma=False
    )
```

```python
import functools
import math

import jax
import jax.numpy as jnp
from jax import lax
from jax.experimental import pallas as pl
from jax.experimental.pallas import tpu as pltpu
from jax.sharding import PartitionSpec as P

HEADS = 8
AHEAD = 4
HELD = 2
RELAY_LAG = 7
VIA = 6
HELD_LAST = 3
LEAD_OWN = 3
LAG_GRADS = 3
LAG_FIRST = 2
LAG_SUMS = 10
BIG = 1e30
MESH = pl.DeviceIdType.MESH
NT = (((1,), (1,)), ((), ()))
TN = (((0,), (0,)), ((), ()))
NN = (((1,), (0,)), ((), ()))


def dot(a, b, dims):
    return lax.dot_general(a, b, dims, preferred_element_type=jnp.float32)


def kernel(
    frames, blocks, block_len, head_dim,
    k_in, v_in, q_in, g_in, mask_in, valid_in,
    dq_ref, dk_ref, dv_ref,
    kv, qg, bias, gate, e_all, d_all, peaks, stat, stat_far, dq_home, dk_home, dv_home,
    dq_out, dq_far, dkv_out, dkv_far, relay, qg_relay,
    mask_ref, valid_ref, own_sem, kv_send, kv_recv, qg_send, qg_recv, gate_sem, stat_send, stat_recv, dq_send, dq_recv, dkv_send, dkv_recv, relay_recv, relay_send, via_recv, via_send,
):
    n = block_len
    t = lax.axis_index("tm")
    s = lax.axis_index("seq")
    scale = head_dim ** (-0.5)
    scale2 = scale * math.log2(math.e)
    left, right = s > 0, s < blocks - 1
    earlier, later = t > 0, t < frames - 1
    sides = ((left, -1), (right, 1))

    def cols(h):
        return pl.ds(pl.multiple_of(h * head_dim, head_dim), head_dim)

    def remote(src, dst, send, recv, dt, ds):
        return pltpu.make_async_remote_copy(
            src_ref=src, dst_ref=dst, send_sem=send, recv_sem=recv,
            device_id=(t + dt, s + ds), device_id_type=MESH,
        )

    def kv_copy(h, side):
        slot = 2 - 2 * side
        return remote(
            kv.at[:, n:2 * n, cols(h)], kv.at[:, slot * n:(slot + 1) * n, cols(h)],
            kv_send.at[side, h], kv_recv.at[side, h], 0, (-1, 1)[side],
        )

    def qg_copy(h):
        return remote(qg.at[:, :n, cols(h)], qg.at[:, n:, cols(h)], qg_send.at[h], qg_recv.at[h], -1, 0)

    def gate_copy():
        return remote(gate.at[0], gate.at[1], gate_sem.at[0], gate_sem.at[1], -1, 0)

    def stat_copy(h, up):
        src, dst = ((slice(0, n), slice(n, 2 * n)), (slice(n, 2 * n), slice(0, n)))[up]
        return remote(
            stat.at[h, :, src], stat_far.at[h, :, dst], stat_send.at[up, h], stat_recv.at[up, h], (-1, 1)[up], 0
        )

    def dq_copy(h):
        return remote(dq_out.at[h], dq_far.at[h], dq_send.at[h], dq_recv.at[h], 1, 0)

    square = frames == 4
    round_about = t == 1 if square else t < 0

    def qg_first(h):
        return remote(qg.at[:, :n, cols(h)], qg_relay.at[h - VIA], qg_send.at[h], via_recv.at[h - VIA], -2, 0)

    def qg_second(h):
        return remote(qg_relay.at[h - VIA], qg.at[:, n:, cols(h)], via_send.at[h - VIA], qg_recv.at[h], 1, 0)

    def dq_first(h):
        return remote(dq_out.at[h], relay.at[h - HELD], dq_send.at[h], relay_recv.at[h - HELD], 2, 0)

    def dq_second(h):
        return remote(relay.at[h - HELD], dq_far.at[h], relay_send.at[h - HELD], dq_recv.at[h], -1, 0)

    def dkv_copy(h, side):
        return remote(
            dkv_out.at[side, h], dkv_far.at[side, h], dkv_send.at[side, h], dkv_recv.at[side, h], 0, (-1, 1)[side]
        )

    def dkv_half(h, side, k):
        rows = slice(k * n, (k + 1) * n)
        return remote(
            dkv_out.at[side, h, rows], dkv_far.at[side, h, rows],
            dkv_send.at[side, h], dkv_recv.at[side, h], 0, (-1, 1)[side],
        )

    barrier = pltpu.get_barrier_semaphore()
    expected = jnp.int32(0)
    for there, dt, ds in ((left, 0, -1), (right, 0, 1), (earlier, -1, 0), (later, 1, 0)):
        expected = expected + there.astype(jnp.int32)

        @pl.when(there)
        def _(dt=dt, ds=ds):
            pl.semaphore_signal(barrier, inc=1, device_id=(t + dt, s + ds), device_id_type=MESH)

    if square:
        expected = expected + jnp.logical_or(round_about, t == 2).astype(jnp.int32)

        @pl.when(t == 0)
        def _():
            pl.semaphore_signal(barrier, inc=1, device_id=(t + 2, s), device_id_type=MESH)

        @pl.when(t == 3)
        def _():
            pl.semaphore_signal(barrier, inc=1, device_id=(t - 2, s), device_id_type=MESH)

    own = [
        pltpu.make_async_copy(k_in.at[0], kv.at[0, n:2 * n], own_sem.at[0]),
        pltpu.make_async_copy(v_in.at[0], kv.at[1, n:2 * n], own_sem.at[1]),
        pltpu.make_async_copy(q_in.at[0], qg.at[0, :n], own_sem.at[2]),
        pltpu.make_async_copy(g_in.at[0], qg.at[1, :n], own_sem.at[3]),
    ]
    small = [
        pltpu.make_async_copy(mask_in, mask_ref, own_sem.at[4]),
        pltpu.make_async_copy(valid_in, valid_ref, own_sem.at[5]),
    ]
    for c in small + own:
        c.start()
    for c in small:
        c.wait()

    for c in range(3):
        gate[0, c:c + 1, :] = jnp.full((1, n), jnp.where(mask_ref[0, 0, 3 + c] == 1, 1.0, 0.0), jnp.float32)

    for c in own:
        c.wait()
    pl.semaphore_wait(barrier, expected)

    @pl.when(earlier)
    def _():
        gate_copy().start()

    if square:
        @pl.when(t == 2)
        def _():
            for h in range(VIA, HEADS):
                qg_first(h).start()

    @pl.loop(0, HEADS)
    def _(h):
        @pl.when(jnp.logical_and(earlier, h < AHEAD))
        def _():
            qg_copy(h).start()

        for side, (there, _) in enumerate(sides):
            @pl.when(there)
            def _(side=side):
                kv_copy(h, side).start()

    row = lax.broadcasted_iota(jnp.int32, (n, n), 0)
    frame_valid = valid_ref[t]

    def key_limit(c):
        near = s + c - 1
        inside = jnp.logical_and(near >= 0, near < blocks).astype(jnp.int32)
        return jnp.maximum(frame_valid - near * n, 0) * inside

    for c in range(3):
        limit = key_limit(c) * jnp.where(mask_ref[0, 0, c] == 1, 1, 0)
        bias[c * n:(c + 1) * n, :n] = jnp.where(row < limit, 0.0, -BIG)

    lane = lax.broadcasted_iota(jnp.int32, (1, 2 * n), 1)
    next_valid = valid_ref[jnp.minimum(t + 1, frames - 1)] * later.astype(jnp.int32)
    okay = jnp.where(lane < jnp.where(lane < n, jnp.minimum(frame_valid - s * n, n), next_valid - s * n + n), 1.0, 0.0)

    zeros = jnp.zeros((n, kv.shape[2]), kv.dtype)
    none = jnp.where(lax.broadcasted_iota(jnp.int32, (2, n), 0) == 0, -BIG, 0.0)
    for slot, there in ((0, left), (2, right)):
        @pl.when(jnp.logical_not(there))
        def _(slot=slot):
            for k in range(2):
                kv[k, slot * n:(slot + 1) * n, :] = zeros
            dkv_far[1 - slot // 2] = jnp.zeros(dkv_far.shape[1:], dkv_far.dtype)

    @pl.when(jnp.logical_not(later))
    def _():
        for k in range(2):
            qg[k, n:, :] = zeros
        gate[1] = jnp.zeros((4, n), jnp.float32)
        for h in range(HEADS):
            stat_far[h, :, n:] = none
            stat[h, :, n:] = jnp.zeros((2, n), jnp.float32)
            peaks[h, :, n:] = jnp.zeros((1, n), jnp.float32)
            e_all[h, :, n:] = jnp.zeros((3 * n, n), jnp.float32)
            d_all[h, :, n:] = jnp.zeros((3 * n, n), jnp.float32)

    @pl.when(jnp.logical_not(earlier))
    def _():
        dq_far[...] = jnp.zeros(dq_far.shape, dq_far.dtype)
        for h in range(HEADS):
            stat_far[h, :, :n] = none

    @pl.when(later)
    def _():
        gate_copy().wait_recv()

    for c in range(3):
        open_here = jnp.logical_and(row < key_limit(c), gate[1, c:c + 1, :] > 0.5)
        bias[c * n:(c + 1) * n, n:] = jnp.where(open_here, 0.0, -BIG)

    def scores(h, half):
        hc = cols(h)
        q = slice(half * n, (half + 1) * n)
        score = dot(kv[0, :, hc], qg[0, q, hc], NT) * scale2 + bias[:, q]
        peak = jnp.max(score, axis=0, keepdims=True)
        e = jnp.exp2(score - peak)
        dprob = dot(kv[1, :, hc], qg[1, q, hc], NT)
        e_all[h, :, q] = e
        d_all[h, :, q] = dprob
        total = jnp.sum(e, axis=0, keepdims=True)
        peaks[h, :, q] = peak
        stat[h, 0:1, q] = peak + jnp.log2(total)
        stat[h, 1:2, q] = jnp.sum(e * dprob, axis=0, keepdims=True) / total

    def own_scores(h):
        for side, (there, _) in enumerate(sides):
            @pl.when(there)
            def _(side=side):
                kv_copy(h, 1 - side).wait_recv()

        scores(h, 0)

        @pl.when(earlier)
        def _():
            stat_copy(h, 0).start()

    def next_scores(h):
        @pl.when(later)
        def _():
            qg_copy(h).wait_recv()
            scores(h, 1)
            stat_copy(h, 1).start()

    def grads(h):
        @pl.when(earlier)
        def _():
            stat_copy(h, 1).wait_recv()

        @pl.when(later)
        def _():
            stat_copy(h, 0).wait_recv()

        hc = cols(h)
        near, far = stat[h], stat_far[h]
        top = jnp.maximum(near[0:1], far[0:1])
        a, b = jnp.exp2(near[0:1] - top), jnp.exp2(far[0:1] - top)
        row_dot = (near[1:2] * a + far[1:2] * b) / (a + b)
        prob = e_all[h] * (okay * jnp.exp2(peaks[h] - (top + jnp.log2(a + b))))
        query, grad, key = qg[0, :, hc], qg[1, :, hc], kv[0, :, hc]

        def send(k, part_of_h):
            home = (dk_home, dv_home)[k]
            home[:, hc] = part_of_h[n:2 * n]
            for side, (there, _) in enumerate(sides):
                part = part_of_h[2 * side * n:(2 * side + 1) * n]
                dkv_out[side, h, k * n:(k + 1) * n] = part.astype(dkv_out.dtype)

                @pl.when(there)
                def _(side=side):
                    dkv_half(h, side, k).start()

        send(1, dot(prob.astype(jnp.bfloat16), grad, NN))
        dscore = (prob * (d_all[h] - row_dot)).astype(jnp.bfloat16)
        send(0, dot(dscore, query, NN) * scale)
        dq = dot(dscore, key, TN) * scale
        dq_home[:, hc] = dq[:n]
        dq_out[h] = dq[n:].astype(dq_out.dtype)

        @pl.when(jnp.logical_and(later, jnp.logical_or(h < HELD, h > HELD_LAST)))
        def _():
            dq_copy(h).start()

        if square:
            @pl.when(jnp.logical_and(round_about, jnp.logical_and(h >= HELD, h <= HELD_LAST)))
            def _():
                dq_first(h).start()

    def sums(h):
        hc = cols(h)

        @pl.when(earlier)
        def _():
            dq_copy(h).wait_recv()

        dq_ref[0, :, hc] = (dq_home[:, hc] + dq_far[h].astype(jnp.float32)).astype(dq_ref.dtype)
        for side, (there, _) in enumerate(sides):
            @pl.when(there)
            def _(side=side):
                dkv_copy(h, 1 - side).wait_recv()
        from_right, from_left = dkv_far[0, h].astype(jnp.float32), dkv_far[1, h].astype(jnp.float32)
        both = from_right + from_left
        dk_ref[0, :, hc] = (dk_home[:, hc] + both[:n]).astype(dk_ref.dtype)
        dv_ref[0, :, hc] = (dv_home[:, hc] + both[n:]).astype(dv_ref.dtype)

    def inputs_sent(h):
        @pl.when(earlier)
        def _():
            qg_copy(h).wait_send()

        for side, (there, _) in enumerate(sides):
            @pl.when(there)
            def _(side=side):
                kv_copy(h, side).wait_send()

    def totals_sent(h):
        @pl.when(earlier)
        def _():
            stat_copy(h, 0).wait_send()

        @pl.when(later)
        def _():
            stat_copy(h, 1).wait_send()

    def grads_sent(h):
        @pl.when(later)
        def _():
            dq_copy(h).wait_send()

        for side, (there, _) in enumerate(sides):
            @pl.when(there)
            def _(side=side):
                dkv_copy(h, side).wait_send()

    @pl.loop(0, LEAD_OWN)
    def _(h):
        own_scores(h)

    lag = jnp.where(earlier, LAG_GRADS, LAG_FIRST)

    @pl.loop(0, HEADS + LAG_SUMS)
    def _(i):
        @pl.when(i < HEADS)
        def _():
            next_scores(i)

        @pl.when(jnp.logical_and(jnp.logical_and(later, jnp.logical_not(round_about)), i == HEADS - 1))
        def _():
            for h in range(HELD, HELD_LAST + 1):
                dq_copy(h).start()

        if square:
            @pl.when(jnp.logical_and(t == 0, i < HEADS - VIA))
            def _():
                qg_first(i + VIA).wait_recv()
                qg_second(i + VIA).start()

        ahead = jnp.where(t == 2, VIA, HEADS) if square else HEADS

        @pl.when(jnp.logical_and(earlier, i < ahead - AHEAD))
        def _():
            qg_copy(i + AHEAD).start()

        @pl.when(jnp.logical_and(i >= lag, i < HEADS + lag))
        def _():
            grads(i - lag)

        if square:
            @pl.when(jnp.logical_and(t == 3, jnp.logical_and(i >= HELD + RELAY_LAG, i <= HELD_LAST + RELAY_LAG)))
            def _():
                dq_first(i - RELAY_LAG).wait_recv()
                dq_second(i - RELAY_LAG).start()

        @pl.when(i < HEADS - LEAD_OWN)
        def _():
            own_scores(i + LEAD_OWN)

        @pl.when(i == HEADS + 1)
        def _():
            @pl.when(earlier)
            def _():
                gate_copy().wait_send()

            @pl.loop(0, HEADS)
            def _(h):
                inputs_sent(h)

        if square:
            @pl.when(jnp.logical_and(t == 3, i == HEADS + LAG_SUMS - 1))
            def _():
                for h in range(HELD, HELD_LAST + 1):
                    dq_second(h).wait_send()

            @pl.when(jnp.logical_and(t == 0, i == HEADS + 1))
            def _():
                for h in range(VIA, HEADS):
                    qg_second(h).wait_send()

        @pl.when(i == HEADS + 2)
        def _():
            @pl.loop(0, HEADS)
            def _(h):
                totals_sent(h)

        @pl.when(i >= LAG_SUMS)
        def _():
            sums(i - LAG_SUMS)
            grads_sent(i - LAG_SUMS)


def store(dq, dk, dv, dq_out, dk_out, dv_out, sem):
    copies = [
        pltpu.make_async_copy(src, dst, sem.at[k])
        for k, (src, dst) in enumerate(((dq, dq_out), (dk, dk_out), (dv, dv_out)))
    ]
    for c in copies:
        c.start()
    for c in copies:
        c.wait()


def solution(mesh):
    frames, blocks = mesh.shape["tm"], mesh.shape["seq"]

    def body(queries, keys, values, grad_out, block_mask, valid_len):
        _, n, feat = queries.shape
        hd = feat // HEADS
        out = jax.ShapeDtypeStruct(queries.shape, queries.dtype)
        vmem = pl.BlockSpec(memory_space=pltpu.VMEM)
        hbm = pl.BlockSpec(memory_space=pl.ANY)
        dma = pltpu.SemaphoreType.DMA
        held = pltpu.VMEM(queries.shape, queries.dtype)
        grads = pl.pallas_call(
            functools.partial(kernel, frames, blocks, n, hd),
            out_shape=(held,) * 3,
            in_specs=[hbm] * 6,
            out_specs=(vmem,) * 3,
            scratch_shapes=[
                pltpu.VMEM((2, 3 * n, feat), jnp.bfloat16),
                pltpu.VMEM((2, 2 * n, feat), jnp.bfloat16),
                pltpu.VMEM((3 * n, 2 * n), jnp.float32),
                pltpu.VMEM((2, 4, n), jnp.float32),
                pltpu.VMEM((HEADS, 3 * n, 2 * n), jnp.float32),
                pltpu.VMEM((HEADS, 3 * n, 2 * n), jnp.float32),
                pltpu.VMEM((HEADS, 1, 2 * n), jnp.float32),
                pltpu.VMEM((HEADS, 2, 2 * n), jnp.float32),
                pltpu.VMEM((HEADS, 2, 2 * n), jnp.float32),
                pltpu.VMEM((n, feat), jnp.float32),
                pltpu.VMEM((n, feat), jnp.float32),
                pltpu.VMEM((n, feat), jnp.float32),
                pltpu.VMEM((HEADS, n, hd), jnp.bfloat16),
                pltpu.VMEM((HEADS, n, hd), jnp.bfloat16),
                pltpu.VMEM((2, HEADS, 2 * n, hd), jnp.bfloat16),
                pltpu.VMEM((2, HEADS, 2 * n, hd), jnp.bfloat16),
                pltpu.VMEM((HELD_LAST + 1 - HELD, n, hd), jnp.bfloat16),
                pltpu.VMEM((HEADS - VIA, 2, n, hd), jnp.bfloat16),
                pltpu.SMEM(block_mask.shape, jnp.int32),
                pltpu.SMEM(valid_len.shape, jnp.int32),
                dma((6,)),
                dma((2, HEADS)),
                dma((2, HEADS)),
                dma((HEADS,)),
                dma((HEADS,)),
                dma((2,)),
                dma((2, HEADS)),
                dma((2, HEADS)),
                dma((HEADS,)),
                dma((HEADS,)),
                dma((2, HEADS)),
                dma((2, HEADS)),
                dma((HELD_LAST + 1 - HELD,)),
                dma((HELD_LAST + 1 - HELD,)),
                dma((HEADS - VIA,)),
                dma((HEADS - VIA,)),
            ],
            compiler_params=pltpu.CompilerParams(collective_id=0, has_side_effects=True),
        )(keys, values, queries, grad_out, block_mask, valid_len)
        return pl.pallas_call(
            store,
            out_shape=(out,) * 3,
            in_specs=[vmem] * 3,
            out_specs=(hbm,) * 3,
            scratch_shapes=[dma((3,))],
        )(*(pltpu.with_memory_space_constraint(x, pltpu.VMEM) for x in grads))

    spec = P("tm", "seq", None)
    return jax.shard_map(
        body, mesh=mesh, in_specs=(spec,) * 5 + (P(),), out_specs=(spec,) * 3, check_vma=False
    )
```

```python
import functools
import math

import jax
import jax.numpy as jnp
from jax import lax
from jax.experimental import pallas as pl
from jax.experimental.pallas import tpu as pltpu
from jax.sharding import PartitionSpec as P

HEADS = 8
AHEAD = 4
HELD = 2
RELAY_LAG = 7
VIA = 5
HELD_LAST = 3
LEAD_OWN = 3
LAG_GRADS = 3
LAG_FIRST = 2
LAG_SUMS = 10
BIG = 1e30
MESH = pl.DeviceIdType.MESH
NT = (((1,), (1,)), ((), ()))
TN = (((0,), (0,)), ((), ()))
NN = (((1,), (0,)), ((), ()))


def dot(a, b, dims):
    return lax.dot_general(a, b, dims, preferred_element_type=jnp.float32)


def kernel(
    frames, blocks, block_len, head_dim,
    k_in, v_in, q_in, g_in, mask_in, valid_in,
    dq_ref, dk_ref, dv_ref,
    kv, qg, bias, gate, e_all, d_all, peaks, stat, stat_far, dq_home, dk_home, dv_home,
    dq_out, dq_far, dkv_out, dkv_far, relay, qg_relay,
    mask_ref, valid_ref, own_sem, kv_send, kv_recv, qg_send, qg_recv, gate_sem, stat_send, stat_recv, dq_send, dq_recv, dkv_send, dkv_recv, relay_recv, relay_send, via_recv, via_send,
):
    n = block_len
    t = lax.axis_index("tm")
    s = lax.axis_index("seq")
    scale = head_dim ** (-0.5)
    scale2 = scale * math.log2(math.e)
    left, right = s > 0, s < blocks - 1
    earlier, later = t > 0, t < frames - 1
    sides = ((left, -1), (right, 1))

    def cols(h):
        return pl.ds(pl.multiple_of(h * head_dim, head_dim), head_dim)

    def remote(src, dst, send, recv, dt, ds):
        return pltpu.make_async_remote_copy(
            src_ref=src, dst_ref=dst, send_sem=send, recv_sem=recv,
            device_id=(t + dt, s + ds), device_id_type=MESH,
        )

    def kv_copy(h, side):
        slot = 2 - 2 * side
        return remote(
            kv.at[:, n:2 * n, cols(h)], kv.at[:, slot * n:(slot + 1) * n, cols(h)],
            kv_send.at[side, h], kv_recv.at[side, h], 0, (-1, 1)[side],
        )

    def qg_copy(h):
        return remote(qg.at[:, :n, cols(h)], qg.at[:, n:, cols(h)], qg_send.at[h], qg_recv.at[h], -1, 0)

    def gate_copy():
        return remote(gate.at[0], gate.at[1], gate_sem.at[0], gate_sem.at[1], -1, 0)

    def stat_copy(h, up):
        src, dst = ((slice(0, n), slice(n, 2 * n)), (slice(n, 2 * n), slice(0, n)))[up]
        return remote(
            stat.at[h, :, src], stat_far.at[h, :, dst], stat_send.at[up, h], stat_recv.at[up, h], (-1, 1)[up], 0
        )

    def dq_copy(h):
        return remote(dq_out.at[h], dq_far.at[h], dq_send.at[h], dq_recv.at[h], 1, 0)

    square = frames == 4
    round_about = t == 1 if square else t < 0

    def qg_first(h):
        return remote(qg.at[:, :n, cols(h)], qg_relay.at[h - VIA], qg_send.at[h], via_recv.at[h - VIA], -2, 0)

    def qg_second(h):
        return remote(qg_relay.at[h - VIA], qg.at[:, n:, cols(h)], via_send.at[h - VIA], qg_recv.at[h], 1, 0)

    def dq_first(h):
        return remote(dq_out.at[h], relay.at[h - HELD], dq_send.at[h], relay_recv.at[h - HELD], 2, 0)

    def dq_second(h):
        return remote(relay.at[h - HELD], dq_far.at[h], relay_send.at[h - HELD], dq_recv.at[h], -1, 0)

    def dkv_copy(h, side):
        return remote(
            dkv_out.at[side, h], dkv_far.at[side, h], dkv_send.at[side, h], dkv_recv.at[side, h], 0, (-1, 1)[side]
        )

    def dkv_half(h, side, k):
        rows = slice(k * n, (k + 1) * n)
        return remote(
            dkv_out.at[side, h, rows], dkv_far.at[side, h, rows],
            dkv_send.at[side, h], dkv_recv.at[side, h], 0, (-1, 1)[side],
        )

    barrier = pltpu.get_barrier_semaphore()
    expected = jnp.int32(0)
    for there, dt, ds in ((left, 0, -1), (right, 0, 1), (earlier, -1, 0), (later, 1, 0)):
        expected = expected + there.astype(jnp.int32)

        @pl.when(there)
        def _(dt=dt, ds=ds):
            pl.semaphore_signal(barrier, inc=1, device_id=(t + dt, s + ds), device_id_type=MESH)

    if square:
        expected = expected + jnp.logical_or(round_about, t == 2).astype(jnp.int32)

        @pl.when(t == 0)
        def _():
            pl.semaphore_signal(barrier, inc=1, device_id=(t + 2, s), device_id_type=MESH)

        @pl.when(t == 3)
        def _():
            pl.semaphore_signal(barrier, inc=1, device_id=(t - 2, s), device_id_type=MESH)

    own = [
        pltpu.make_async_copy(k_in.at[0], kv.at[0, n:2 * n], own_sem.at[0]),
        pltpu.make_async_copy(v_in.at[0], kv.at[1, n:2 * n], own_sem.at[1]),
        pltpu.make_async_copy(q_in.at[0], qg.at[0, :n], own_sem.at[2]),
        pltpu.make_async_copy(g_in.at[0], qg.at[1, :n], own_sem.at[3]),
    ]
    small = [
        pltpu.make_async_copy(mask_in, mask_ref, own_sem.at[4]),
        pltpu.make_async_copy(valid_in, valid_ref, own_sem.at[5]),
    ]
    for c in small + own:
        c.start()
    for c in small:
        c.wait()

    for c in range(3):
        gate[0, c:c + 1, :] = jnp.full((1, n), jnp.where(mask_ref[0, 0, 3 + c] == 1, 1.0, 0.0), jnp.float32)

    for c in own[2:]:
        c.wait()
    pl.semaphore_wait(barrier, expected)

    @pl.when(earlier)
    def _():
        gate_copy().start()

    if square:
        @pl.when(t == 2)
        def _():
            for h in range(VIA, HEADS):
                qg_first(h).start()

    @pl.when(earlier)
    def _():
        for h in range(AHEAD):
            qg_copy(h).start()

    for c in own[:2]:
        c.wait()

    @pl.loop(0, HEADS)
    def _(h):

        for side, (there, _) in enumerate(sides):
            @pl.when(there)
            def _(side=side):
                kv_copy(h, side).start()

    row = lax.broadcasted_iota(jnp.int32, (n, n), 0)
    frame_valid = valid_ref[t]

    def key_limit(c):
        near = s + c - 1
        inside = jnp.logical_and(near >= 0, near < blocks).astype(jnp.int32)
        return jnp.maximum(frame_valid - near * n, 0) * inside

    for c in range(3):
        limit = key_limit(c) * jnp.where(mask_ref[0, 0, c] == 1, 1, 0)
        bias[c * n:(c + 1) * n, :n] = jnp.where(row < limit, 0.0, -BIG)

    lane = lax.broadcasted_iota(jnp.int32, (1, 2 * n), 1)
    next_valid = valid_ref[jnp.minimum(t + 1, frames - 1)] * later.astype(jnp.int32)
    okay = jnp.where(lane < jnp.where(lane < n, jnp.minimum(frame_valid - s * n, n), next_valid - s * n + n), 1.0, 0.0)

    zeros = jnp.zeros((n, kv.shape[2]), kv.dtype)
    none = jnp.where(lax.broadcasted_iota(jnp.int32, (2, n), 0) == 0, -BIG, 0.0)
    for slot, there in ((0, left), (2, right)):
        @pl.when(jnp.logical_not(there))
        def _(slot=slot):
            for k in range(2):
                kv[k, slot * n:(slot + 1) * n, :] = zeros
            dkv_far[1 - slot // 2] = jnp.zeros(dkv_far.shape[1:], dkv_far.dtype)

    @pl.when(jnp.logical_not(later))
    def _():
        for k in range(2):
            qg[k, n:, :] = zeros
        gate[1] = jnp.zeros((4, n), jnp.float32)
        for h in range(HEADS):
            stat_far[h, :, n:] = none
            stat[h, :, n:] = jnp.zeros((2, n), jnp.float32)
            peaks[h, :, n:] = jnp.zeros((1, n), jnp.float32)
            e_all[h, :, n:] = jnp.zeros((3 * n, n), jnp.float32)
            d_all[h, :, n:] = jnp.zeros((3 * n, n), jnp.float32)

    @pl.when(jnp.logical_not(earlier))
    def _():
        dq_far[...] = jnp.zeros(dq_far.shape, dq_far.dtype)
        for h in range(HEADS):
            stat_far[h, :, :n] = none

    @pl.when(later)
    def _():
        gate_copy().wait_recv()

    for c in range(3):
        open_here = jnp.logical_and(row < key_limit(c), gate[1, c:c + 1, :] > 0.5)
        bias[c * n:(c + 1) * n, n:] = jnp.where(open_here, 0.0, -BIG)

    def scores(h, half):
        hc = cols(h)
        q = slice(half * n, (half + 1) * n)
        score = dot(kv[0, :, hc], qg[0, q, hc], NT) * scale2 + bias[:, q]
        peak = jnp.max(score, axis=0, keepdims=True)
        e = jnp.exp2(score - peak)
        dprob = dot(kv[1, :, hc], qg[1, q, hc], NT)
        e_all[h, :, q] = e
        d_all[h, :, q] = dprob
        total = jnp.sum(e, axis=0, keepdims=True)
        peaks[h, :, q] = peak
        stat[h, 0:1, q] = peak + jnp.log2(total)
        stat[h, 1:2, q] = jnp.sum(e * dprob, axis=0, keepdims=True) / total

    def own_scores(h):
        for side, (there, _) in enumerate(sides):
            @pl.when(there)
            def _(side=side):
                kv_copy(h, 1 - side).wait_recv()

        scores(h, 0)

        @pl.when(earlier)
        def _():
            stat_copy(h, 0).start()

    def next_scores(h):
        @pl.when(later)
        def _():
            qg_copy(h).wait_recv()
            scores(h, 1)
            stat_copy(h, 1).start()

    def grads(h):
        @pl.when(earlier)
        def _():
            stat_copy(h, 1).wait_recv()

        @pl.when(later)
        def _():
            stat_copy(h, 0).wait_recv()

        hc = cols(h)
        near, far = stat[h], stat_far[h]
        top = jnp.maximum(near[0:1], far[0:1])
        a, b = jnp.exp2(near[0:1] - top), jnp.exp2(far[0:1] - top)
        row_dot = (near[1:2] * a + far[1:2] * b) / (a + b)
        prob = e_all[h] * (okay * jnp.exp2(peaks[h] - (top + jnp.log2(a + b))))
        query, grad, key = qg[0, :, hc], qg[1, :, hc], kv[0, :, hc]

        def send(k, part_of_h):
            home = (dk_home, dv_home)[k]
            home[:, hc] = part_of_h[n:2 * n]
            for side, (there, _) in enumerate(sides):
                part = part_of_h[2 * side * n:(2 * side + 1) * n]
                dkv_out[side, h, k * n:(k + 1) * n] = part.astype(dkv_out.dtype)

                @pl.when(there)
                def _(side=side):
                    dkv_half(h, side, k).start()

        send(1, dot(prob.astype(jnp.bfloat16), grad, NN))
        dscore = (prob * (d_all[h] - row_dot)).astype(jnp.bfloat16)
        send(0, dot(dscore, query, NN) * scale)
        dq = dot(dscore, key, TN) * scale
        dq_home[:, hc] = dq[:n]
        dq_out[h] = dq[n:].astype(dq_out.dtype)

        @pl.when(jnp.logical_and(later, jnp.logical_or(h < HELD, h > HELD_LAST)))
        def _():
            dq_copy(h).start()

        if square:
            @pl.when(jnp.logical_and(round_about, jnp.logical_and(h >= HELD, h <= HELD_LAST)))
            def _():
                dq_first(h).start()

    def sums(h):
        hc = cols(h)

        @pl.when(earlier)
        def _():
            dq_copy(h).wait_recv()

        dq_ref[0, :, hc] = (dq_home[:, hc] + dq_far[h].astype(jnp.float32)).astype(dq_ref.dtype)
        for side, (there, _) in enumerate(sides):
            @pl.when(there)
            def _(side=side):
                dkv_copy(h, 1 - side).wait_recv()
        from_right, from_left = dkv_far[0, h].astype(jnp.float32), dkv_far[1, h].astype(jnp.float32)
        both = from_right + from_left
        dk_ref[0, :, hc] = (dk_home[:, hc] + both[:n]).astype(dk_ref.dtype)
        dv_ref[0, :, hc] = (dv_home[:, hc] + both[n:]).astype(dv_ref.dtype)

    def inputs_sent(h):
        @pl.when(earlier)
        def _():
            qg_copy(h).wait_send()

        for side, (there, _) in enumerate(sides):
            @pl.when(there)
            def _(side=side):
                kv_copy(h, side).wait_send()

    def totals_sent(h):
        @pl.when(earlier)
        def _():
            stat_copy(h, 0).wait_send()

        @pl.when(later)
        def _():
            stat_copy(h, 1).wait_send()

    def grads_sent(h):
        @pl.when(later)
        def _():
            dq_copy(h).wait_send()

        for side, (there, _) in enumerate(sides):
            @pl.when(there)
            def _(side=side):
                dkv_copy(h, side).wait_send()

    @pl.loop(0, LEAD_OWN)
    def _(h):
        own_scores(h)

    lag = jnp.where(earlier, LAG_GRADS, LAG_FIRST)

    @pl.loop(0, HEADS + LAG_SUMS)
    def _(i):
        @pl.when(i < HEADS)
        def _():
            next_scores(i)

        @pl.when(jnp.logical_and(jnp.logical_and(later, jnp.logical_not(round_about)), i == HEADS - 1))
        def _():
            for h in range(HELD, HELD_LAST + 1):
                dq_copy(h).start()

        if square:
            @pl.when(jnp.logical_and(t == 0, i < HEADS - VIA))
            def _():
                qg_first(i + VIA).wait_recv()
                qg_second(i + VIA).start()

        ahead = jnp.where(t == 2, VIA, HEADS) if square else HEADS

        @pl.when(jnp.logical_and(earlier, i < ahead - AHEAD))
        def _():
            qg_copy(i + AHEAD).start()

        @pl.when(jnp.logical_and(i >= lag, i < HEADS + lag))
        def _():
            grads(i - lag)

        if square:
            @pl.when(jnp.logical_and(t == 3, jnp.logical_and(i >= HELD + RELAY_LAG, i <= HELD_LAST + RELAY_LAG)))
            def _():
                dq_first(i - RELAY_LAG).wait_recv()
                dq_second(i - RELAY_LAG).start()

        @pl.when(i < HEADS - LEAD_OWN)
        def _():
            own_scores(i + LEAD_OWN)

        @pl.when(i == HEADS + 1)
        def _():
            @pl.when(earlier)
            def _():
                gate_copy().wait_send()

            @pl.loop(0, HEADS)
            def _(h):
                inputs_sent(h)

        if square:
            @pl.when(jnp.logical_and(t == 3, i == HEADS + LAG_SUMS - 1))
            def _():
                for h in range(HELD, HELD_LAST + 1):
                    dq_second(h).wait_send()

            @pl.when(jnp.logical_and(t == 0, i == HEADS + 1))
            def _():
                for h in range(VIA, HEADS):
                    qg_second(h).wait_send()

        @pl.when(i == HEADS + 2)
        def _():
            @pl.loop(0, HEADS)
            def _(h):
                totals_sent(h)

        @pl.when(i >= LAG_SUMS)
        def _():
            sums(i - LAG_SUMS)
            grads_sent(i - LAG_SUMS)


def store(dq, dk, dv, dq_out, dk_out, dv_out, sem):
    copies = [
        pltpu.make_async_copy(src, dst, sem.at[k])
        for k, (src, dst) in enumerate(((dq, dq_out), (dk, dk_out), (dv, dv_out)))
    ]
    for c in copies:
        c.start()
    for c in copies:
        c.wait()


def solution(mesh):
    frames, blocks = mesh.shape["tm"], mesh.shape["seq"]

    def body(queries, keys, values, grad_out, block_mask, valid_len):
        _, n, feat = queries.shape
        hd = feat // HEADS
        out = jax.ShapeDtypeStruct(queries.shape, queries.dtype)
        vmem = pl.BlockSpec(memory_space=pltpu.VMEM)
        hbm = pl.BlockSpec(memory_space=pl.ANY)
        dma = pltpu.SemaphoreType.DMA
        held = pltpu.VMEM(queries.shape, queries.dtype)
        grads = pl.pallas_call(
            functools.partial(kernel, frames, blocks, n, hd),
            out_shape=(held,) * 3,
            in_specs=[hbm] * 6,
            out_specs=(vmem,) * 3,
            scratch_shapes=[
                pltpu.VMEM((2, 3 * n, feat), jnp.bfloat16),
                pltpu.VMEM((2, 2 * n, feat), jnp.bfloat16),
                pltpu.VMEM((3 * n, 2 * n), jnp.float32),
                pltpu.VMEM((2, 4, n), jnp.float32),
                pltpu.VMEM((HEADS, 3 * n, 2 * n), jnp.float32),
                pltpu.VMEM((HEADS, 3 * n, 2 * n), jnp.float32),
                pltpu.VMEM((HEADS, 1, 2 * n), jnp.float32),
                pltpu.VMEM((HEADS, 2, 2 * n), jnp.float32),
                pltpu.VMEM((HEADS, 2, 2 * n), jnp.float32),
                pltpu.VMEM((n, feat), jnp.float32),
                pltpu.VMEM((n, feat), jnp.float32),
                pltpu.VMEM((n, feat), jnp.float32),
                pltpu.VMEM((HEADS, n, hd), jnp.bfloat16),
                pltpu.VMEM((HEADS, n, hd), jnp.bfloat16),
                pltpu.VMEM((2, HEADS, 2 * n, hd), jnp.bfloat16),
                pltpu.VMEM((2, HEADS, 2 * n, hd), jnp.bfloat16),
                pltpu.VMEM((HELD_LAST + 1 - HELD, n, hd), jnp.bfloat16),
                pltpu.VMEM((HEADS - VIA, 2, n, hd), jnp.bfloat16),
                pltpu.SMEM(block_mask.shape, jnp.int32),
                pltpu.SMEM(valid_len.shape, jnp.int32),
                dma((6,)),
                dma((2, HEADS)),
                dma((2, HEADS)),
                dma((HEADS,)),
                dma((HEADS,)),
                dma((2,)),
                dma((2, HEADS)),
                dma((2, HEADS)),
                dma((HEADS,)),
                dma((HEADS,)),
                dma((2, HEADS)),
                dma((2, HEADS)),
                dma((HELD_LAST + 1 - HELD,)),
                dma((HELD_LAST + 1 - HELD,)),
                dma((HEADS - VIA,)),
                dma((HEADS - VIA,)),
            ],
            compiler_params=pltpu.CompilerParams(collective_id=0, has_side_effects=True),
        )(keys, values, queries, grad_out, block_mask, valid_len)
        return pl.pallas_call(
            store,
            out_shape=(out,) * 3,
            in_specs=[vmem] * 3,
            out_specs=(hbm,) * 3,
            scratch_shapes=[dma((3,))],
        )(*(pltpu.with_memory_space_constraint(x, pltpu.VMEM) for x in grads))

    spec = P("tm", "seq", None)
    return jax.shard_map(
        body, mesh=mesh, in_specs=(spec,) * 5 + (P(),), out_specs=(spec,) * 3, check_vma=False
    )
```
